32 devices in a mesh: grp: 2 (over x), seq: 16 (over z, y, core).
Axes of the slice: x: 2, y: 2, z: 4, core: 2. Of those that a mesh axis runs over, the one named last changes fastest.
Arguments:
- query_stream: bfloat16 [4096, 2048], P(('grp', 'seq')), parts along dimension 0, may hold values from -6 to 6
- key_stream: bfloat16 [4096, 2048], P(('grp', 'seq')), parts along dimension 0, may hold values from -6 to 6
- value_stream: bfloat16 [4096, 2048], P(('grp', 'seq')), parts along dimension 0, may hold values from -6 to 6
- cotangent: bfloat16 [4096, 2048], P(('grp', 'seq')), parts along dimension 0, may hold values from -6 to 6
- decay_rate: float32 [128, 16], replicated, may hold values from 0 to 1, as said below
- residue: float32 [128, 16], replicated, may hold values from -4 to 4
Outputs:
- mixer_out: bfloat16 [4096, 2048], P(('grp', 'seq')), parts along dimension 0
- query_grad: bfloat16 [4096, 2048], P(('grp', 'seq')), parts along dimension 0
- key_grad: bfloat16 [4096, 2048], P(('grp', 'seq')), parts along dimension 0
- value_grad: bfloat16 [4096, 2048], P(('grp', 'seq')), parts along dimension 0
- filter_grad: float32 [256, 16], P('grp'), parts along dimension 0
The draws below stay inside these ranges and needn't reach their ends.
There are 2 independent parts, one for each index of `grp`. The reference program is written for one: setup_inputs(seed, part) draws one part's arguments, and reference() takes and returns one part's arrays. A program takes and returns all parts, laid end to end along the dimension named above; an argument that names none is the same for every part. Nothing has to cross between parts.
Inputs may be any that keep to these rules, and one draw needn't show every extreme that they name: `decay_rate`: positive decay rates.
All inputs are finite; a program needn't handle non-finite values.
Results may differ from the reference program's by a relative error of at most 0.0023.
Values sent between devices are 32-bit elements; how exact they have to be, the bound alone decides.
No kernel may reach another device: no remote copies, remote signals or barrier semaphores. Data moves between devices by JAX's collectives and lax.ppermute only.
A program may use at most 192 MiB of HBM per device.

```python
import math
import jax
import jax.numpy as jnp
from jax import lax

D = 2048
N = 16
TOK_DEV = 128
G = 128
TOKENS = 2048


def draw_decay_rate(key, part):
    key_pick = jax.random.fold_in(key, 11)
    key_slow = jax.random.fold_in(key, 12)
    key_fast = jax.random.fold_in(key, 13)
    share = 0.5
    picked = jax.random.uniform(key_pick, (G, N), jnp.float32) < share
    slow_rate = jnp.exp(jax.random.uniform(key_slow, (G, N), jnp.float32, math.log(0.1 / TOKENS), math.log(2.0 / TOKENS)))
    fast_rate = jnp.exp(jax.random.uniform(key_fast, (G, N), jnp.float32, math.log(1.0 / 64.0), math.log(1.0 / 16.0)))
    return jnp.where(picked, fast_rate, slow_rate).astype(jnp.float32)


def steps_of(key, dims, split, least, top_value):
    level = 1.0
    for position, blocks in split:
        heights = jax.random.uniform(jax.random.fold_in(jax.random.fold_in(key, 6), position), (blocks,), jnp.float32, least / len(split), top_value / len(split))
        level = level * jnp.repeat(jnp.exp(heights), dims[position] // blocks).reshape((-1,) + (1,) * (len(dims) - 1 - position))
    return level


def bell_draw(stream_key, extent, spread, reach, split=(), kind=jnp.bfloat16):
    factor_of = steps_of(stream_key, extent, split, -0.22, 0.18) if split else 1.0
    array = jax.random.normal(stream_key, extent, jnp.float32) * spread * factor_of
    return jnp.minimum(jnp.maximum(array, -reach), reach).astype(kind)


def setup_inputs(seed: int = 0, part: int = 0) -> dict:
    seeds = jax.random.split(jax.random.key(seed), 7)
    part_keys = jax.random.split(jax.random.fold_in(seeds[6], part), 7)
    query_stream = bell_draw(part_keys[0], (TOKENS, D), 1.0, 6.0, ((0, 16),))
    key_stream = bell_draw(part_keys[1], (TOKENS, D), 1.0, 6.0, ((0, 16),))
    value_stream = bell_draw(part_keys[2], (TOKENS, D), 1.0, 6.0, ((0, 16),))
    cotangent = bell_draw(part_keys[3], (TOKENS, D), 1.0, 6.0, ((0, 16),))
    decay_rate = draw_decay_rate(jax.random.fold_in(seeds[6], 71), part)
    residue = bell_draw(seeds[5], (G, N), 1.0, 4.0, (), jnp.float32)
    return dict(query_stream=query_stream, key_stream=key_stream, value_stream=value_stream, cotangent=cotangent, decay_rate=decay_rate, residue=residue)


PRECISE = lax.Precision.HIGHEST

def mixer(key_full, value_full, residue, decay_rate):
    length = TOK_DEV
    blocks = TOKENS // TOK_DEV
    groups, modes = decay_rate.shape
    width = key_full.shape[1]
    per_group = width // groups
    positions = jnp.arange(length, dtype=jnp.float32)
    weights = residue * jnp.sqrt(2.0 * decay_rate / modes)
    decay_grid = decay_rate[:, :, None]
    lag_filter = jnp.einsum('gn,gnl->gl', weights, jnp.exp(-decay_grid * positions), precision=PRECISE)
    lag_index = jnp.arange(length, dtype=jnp.int32)[:, None] - jnp.arange(length, dtype=jnp.int32)[None, :]
    toeplitz = jnp.where((lag_index >= 0)[None], lag_filter[:, jnp.maximum(lag_index, 0)], 0.0)
    gated = (key_full * value_full).reshape(blocks, length, groups, per_group)
    local_part = jnp.einsum('gts,bsgk->btgk', toeplitz, gated, precision=PRECISE)
    end_powers = jnp.exp(-decay_grid * (length - 1.0 - positions))
    end_state = jnp.einsum('gnt,btgk->bgkn', end_powers, gated, precision=PRECISE)
    block_power = jnp.exp(-decay_rate * length)[:, None, :]

    def advance(state_now, block_end):
        return (state_now * block_power + block_end, state_now)
    initial = jnp.zeros((groups, per_group, modes), jnp.float32)
    final_state, incoming = lax.scan(advance, initial, end_state)
    forward_coef = weights[:, :, None] * jnp.exp(-decay_grid * (positions + 1.0))
    carried = jnp.einsum('gnt,bgkn->btgk', forward_coef, incoming, precision=PRECISE)
    return (local_part + carried).reshape(TOKENS, width)

def reference(query_stream, key_stream, value_stream, cotangent, decay_rate, residue):
    query_full = query_stream.astype(jnp.float32)
    key_full = key_stream.astype(jnp.float32)
    value_full = value_stream.astype(jnp.float32)

    def product(query_in, key_in, value_in, residue_in):
        return query_in * mixer(key_in, value_in, residue_in, decay_rate)
    output_value, pullback = jax.vjp(product, query_full, key_full, value_full, residue)
    gradients = pullback(cotangent.astype(jnp.float32))
    filter_grad = gradients[3] / math.sqrt(TOKENS)
    return (output_value.astype(jnp.bfloat16), gradients[0].astype(jnp.bfloat16), gradients[1].astype(jnp.bfloat16), gradients[2].astype(jnp.bfloat16), filter_grad)
```

```python
import functools
import math

import jax
import jax.numpy as jnp
from jax import lax
from jax.experimental import pallas as pl
from jax.experimental.pallas import tpu as pltpu
from jax.sharding import PartitionSpec as P

PER = 16
MODES = 16
LANES = 128
PACK = LANES // PER
F32 = jnp.float32
BF16 = jnp.bfloat16


def lane_iota(shape):
    return lax.broadcasted_iota(jnp.int32, shape, 1)


def row_iota(shape):
    return lax.broadcasted_iota(jnp.int32, shape, 0)


def split(value):
    high = value.astype(BF16)
    return high, (value - high.astype(F32)).astype(BF16)


def dot3(left, right):
    left_high, left_low = split(left)
    right_high, right_low = split(right)
    return jnp.dot(
        jnp.concatenate([left_high, left_high, left_low], axis=1),
        jnp.concatenate([right_high, right_low, right_high], axis=0),
        preferred_element_type=F32,
    )


def own_group(stack):
    group = lane_iota((MODES, LANES)) // PER
    total = jnp.zeros((MODES, LANES), F32)
    for g in range(PACK):
        total = total + jnp.where(group == g, stack[g * MODES : (g + 1) * MODES], 0.0)
    return total


def columns(transposed, block):
    return jnp.concatenate(
        [
            jnp.broadcast_to(transposed[:MODES, g : g + 1], (MODES, LANES))
            for g in range(block * PACK, (block + 1) * PACK)
        ],
        axis=0,
    )


def group_rows(product):
    width = product.shape[1]
    count = width // LANES
    tall = jnp.concatenate([product[:, i * LANES : (i + 1) * LANES] for i in range(count)], axis=0)
    high, low = split(tall)
    same = (lane_iota((LANES, LANES)) // PER == row_iota((LANES, LANES)) // PER).astype(F32)
    sums = jnp.dot(
        jnp.concatenate([high, low], axis=1),
        jnp.concatenate([same, same], axis=0).astype(BF16),
        preferred_element_type=F32,
    )
    pick = lane_iota((MODES, LANES)) % PER == row_iota((MODES, LANES))
    rows = [
        jnp.sum(jnp.where(pick, sums[i * MODES : (i + 1) * MODES], 0.0), axis=0, keepdims=True)
        for i in range(count)
    ]
    return jnp.concatenate(rows, axis=1)


def position():
    return lax.axis_index("seq")


def bit_of(index, mask):
    return (index & mask) != 0


def params(limit=48):
    return pltpu.CompilerParams(vmem_limit_bytes=limit << 20)


def states_kernel(k_ref, v_ref, q_ref, c_ref, decay_ref, send_ref, keep_ref, rate_ref, pad_ref):
    step = pl.program_id(0)
    length, width = k_ref.shape
    groups = decay_ref.shape[0]
    pad_ref[:groups, :MODES] = decay_ref[...]
    transposed = pad_ref[...].T
    time = lane_iota((LANES, length)).astype(F32)
    ends = []
    starts = []
    rates = []
    for block in range(width // LANES):
        lanes = slice(block * LANES, (block + 1) * LANES)
        rate = columns(transposed, block)
        gated = k_ref[:, lanes].astype(F32) * v_ref[:, lanes].astype(F32)
        upstream = q_ref[:, lanes].astype(F32) * c_ref[:, lanes].astype(F32)
        ends.append(own_group(dot3(jnp.exp(-rate * (length - 1.0 - time)), gated)))
        starts.append(own_group(dot3(jnp.exp(-rate * time), upstream)))
        rates.append(own_group(rate))
    rate_ref[...] = jnp.concatenate(rates, axis=1)
    both = jnp.concatenate(
        [jnp.concatenate(ends, axis=1), jnp.concatenate(starts, axis=1)], axis=0
    )
    steps = pl.num_programs(0)
    mine = (step >= steps // 2) == bit_of(position(), 1)
    place = pl.ds(pl.multiple_of((step % (steps // 2)) * width, width), width)

    @pl.when(mine)
    def _():
        keep_ref[:, place] = both

    @pl.when(jnp.logical_not(mine))
    def _():
        send_ref[:, place] = both


def states(k, v, q, c, decay):
    length, total = k.shape
    groups = decay.shape[0]
    steps = 4
    width = total // steps
    stream = pl.BlockSpec((length, width), lambda i: (0, i))
    whole = pl.BlockSpec((2 * MODES, total // 2), lambda i: (0, 0))
    return pl.pallas_call(
        states_kernel,
        grid=(steps,),
        in_specs=[stream] * 4 + [pl.BlockSpec((groups // steps, MODES), lambda i: (i, 0))],
        out_specs=[whole, whole, pl.BlockSpec((MODES, width), lambda i: (0, i))],
        out_shape=[
            jax.ShapeDtypeStruct((2 * MODES, total // 2), F32),
            jax.ShapeDtypeStruct((2 * MODES, total // 2), F32),
            jax.ShapeDtypeStruct((MODES, total), F32),
        ],
        scratch_shapes=[pltpu.VMEM((LANES, LANES), F32)],
        compiler_params=params(),
        name="states",
    )(k, v, q, c, decay)


def tables_kernel(length, decay_ref, residue_ref, weight_ref, fh_ref, fl_ref, bh_ref, bl_ref, pad_ref):
    groups = decay_ref.shape[0]
    width = weight_ref.shape[1]
    pad_ref[:groups, :MODES] = decay_ref[...]
    rates = pad_ref[...].T
    pad_ref[:groups, :MODES] = residue_ref[...] * jnp.sqrt(2.0 * decay_ref[...] / MODES)
    weights = pad_ref[...].T
    time = lane_iota((LANES, length)).astype(F32)
    for block in range(width // LANES):
        lanes = slice(block * LANES, (block + 1) * LANES)
        rate = columns(rates, block)
        weight = columns(weights, block)
        weight_ref[:, lanes] = own_group(weight)
        high, low = split((weight * jnp.exp(-rate * (time + 1.0))).T)
        fh_ref[:, lanes] = high
        fl_ref[:, lanes] = low
        high, low = split((weight * jnp.exp(-rate * (length - time))).T)
        bh_ref[:, lanes] = high
        bl_ref[:, lanes] = low


def tables(decay, residue, length):
    groups = decay.shape[0]
    total = groups * PER
    steps = 4
    small = pl.BlockSpec((groups // steps, MODES), lambda i: (i, 0))
    tall = pl.BlockSpec((length, total // steps), lambda i: (0, i))
    return pl.pallas_call(
        functools.partial(tables_kernel, length),
        grid=(steps,),
        in_specs=[small, small],
        out_specs=[pl.BlockSpec((MODES, total // steps), lambda i: (0, i))] + [tall] * 4,
        out_shape=[jax.ShapeDtypeStruct((MODES, total), F32)]
        + [jax.ShapeDtypeStruct((length, total), BF16)] * 4,
        scratch_shapes=[pltpu.VMEM((LANES, LANES), F32)],
        compiler_params=params(),
        name="tables",
    )(decay, residue)


def lag_kernel(k_ref, v_ref, q_ref, c_ref, rate_ref, out_ref, gated_ref, upstream_ref):
    step = pl.program_id(0)
    length, width = k_ref.shape
    gated_ref[...] = k_ref[...].astype(F32) * v_ref[...].astype(F32)
    upstream_ref[...] = q_ref[...].astype(F32) * c_ref[...].astype(F32)
    decay = jnp.exp(-rate_ref[...])

    def eight(i, carry):
        state, total = carry
        base = pl.multiple_of(i * 8, 8)
        x_rows = gated_ref[pl.ds(base, 8), :]
        u_rows = upstream_ref[pl.ds(base, 8), :]
        for j in range(8):
            state = state * decay + jnp.broadcast_to(x_rows[j : j + 1], (MODES, width))
            total = total + state * jnp.broadcast_to(u_rows[j : j + 1], (MODES, width))
        return state, total

    zero = jnp.zeros((MODES, width), F32)
    _, total = lax.fori_loop(0, length // 8, eight, (zero, zero))
    out_ref[pl.ds(step, 1), :] = group_rows(total)


def lag_part(k, v, q, c, rate):
    length, total = k.shape
    steps = 4
    width = total // steps
    stream = pl.BlockSpec((length, width), lambda i: (0, i))
    return pl.pallas_call(
        lag_kernel,
        grid=(steps,),
        in_specs=[stream] * 4 + [pl.BlockSpec((MODES, width), lambda i: (0, i))],
        out_specs=pl.BlockSpec((8, width), lambda i: (0, 0)),
        out_shape=jax.ShapeDtypeStruct((8, width), F32),
        scratch_shapes=[pltpu.VMEM((length, width), F32)] * 2,
        compiler_params=params(),
        name="lag_part",
    )(k, v, q, c, rate)


def fold(first, second, shift, row):
    low = (row & shift) == 0
    kept = jnp.where(low, first, second)
    moved = jnp.where(low, second, first)
    return kept + pltpu.roll(moved, shift, 0)


def scan_kernel(reverse, a_ref, b_ref, rate_ref, weight_ref, out_ref, in_ref):
    length, width = a_ref.shape
    in_ref[...] = a_ref[...].astype(F32) * b_ref[...].astype(F32)
    decay = jnp.exp(-rate_ref[...])
    weight = weight_ref[...]
    row = row_iota((8, width))

    def eight(i, state):
        at = length // 8 - 1 - i if reverse else i
        base = pl.multiple_of(at * 8, 8)
        rows = in_ref[pl.ds(base, 8), :]
        parts = [None] * 8
        for j in reversed(range(8)) if reverse else range(8):
            state = state * decay + jnp.broadcast_to(rows[j : j + 1], (MODES, width))
            product = state * weight
            parts[j] = product[:8] + product[8:]
        four = [fold(parts[2 * j], parts[2 * j + 1], 1, row) for j in range(4)]
        two = [fold(four[2 * j], four[2 * j + 1], 2, row) for j in range(2)]
        out_ref[pl.ds(base, 8), :] = fold(two[0], two[1], 4, row)
        return state

    lax.fori_loop(0, length // 8, eight, jnp.zeros((MODES, width), F32))


def scan_part(a, b, rate, weight, reverse):
    length, total = a.shape
    steps = 4
    width = total // steps
    stream = pl.BlockSpec((length, width), lambda i: (0, i))
    wide = pl.BlockSpec((MODES, width), lambda i: (0, i))
    return pl.pallas_call(
        functools.partial(scan_kernel, reverse),
        grid=(steps,),
        in_specs=[stream, stream, wide, wide],
        out_specs=stream,
        out_shape=jax.ShapeDtypeStruct((length, total), F32),
        scratch_shapes=[pltpu.VMEM((length, width), F32)],
        compiler_params=params(),
        name="scan_back" if reverse else "scan_fore",
    )(a, b, rate, weight)


def join(own, other, late, power, step_decay):
    own_end, own_start = own[:MODES], own[MODES : 2 * MODES]
    other_end, other_start = other[:MODES], other[MODES : 2 * MODES]
    early_end = jnp.where(late, other_end, own_end)
    late_end = jnp.where(late, own_end, other_end)
    early_start = jnp.where(late, other_start, own_start)
    late_start = jnp.where(late, own_start, other_start)
    end = late_end + power * early_end
    start = early_start + power * late_start
    return end, start, early_end * late_start * step_decay


def pass_down(first, second, before, after, power):
    early = (before, second + power * after)
    late = (first + power * before, after)
    return early, late


def quarter_of(index, half):
    both = (index & 1) * 2 + ((index >> 1) & 1)
    return pl.ds(pl.multiple_of(both * half, half), half)


def core_kernel(length, own_ref, other_ref, rate_ref, send_ref, keep_ref, lag_ref):
    index = position()
    half = own_ref.shape[1]
    quarter = half // 2
    place = pl.ds(pl.multiple_of((index & 1) * half, half), half)
    rate = rate_ref[:, place]
    end, start, cross = join(
        own_ref[...],
        other_ref[...],
        bit_of(index, 1),
        jnp.exp(-rate * length),
        jnp.exp(-rate),
    )
    both = jnp.concatenate([end, start], axis=0)
    second = bit_of(index, 2)
    keep_ref[...] = jnp.where(second, both[:, quarter:], both[:, :quarter])
    send_ref[...] = jnp.where(second, both[:, :quarter], both[:, quarter:])
    rows = group_rows(cross)
    lag_ref[0:1, :] = rows[:, :quarter]
    lag_ref[1:2, :] = rows[:, quarter:]


def core_join(length, own, other, rate):
    half = own.shape[1]
    return pl.pallas_call(
        functools.partial(core_kernel, length),
        out_shape=[
            jax.ShapeDtypeStruct((2 * MODES, half // 2), F32),
            jax.ShapeDtypeStruct((2 * MODES, half // 2), F32),
            jax.ShapeDtypeStruct((8, half // 2), F32),
        ],
        compiler_params=params(),
        name="core_join",
    )(own, other, rate)


def plane_kernel(length, own_ref, other_ref, lag_ref, core_lag_ref, rate_ref, out_ref):
    index = position()
    rate = rate_ref[:, quarter_of(index, own_ref.shape[1])]
    end, start, cross = join(
        own_ref[...],
        other_ref[...],
        bit_of(index, 2),
        jnp.exp(-rate * (2 * length)),
        jnp.exp(-rate),
    )
    out_ref[:MODES] = end
    out_ref[MODES : 2 * MODES] = start
    base = 2 * MODES
    out_ref[base : base + 4] = lag_ref[0:4]
    out_ref[base + 4 : base + 6] = core_lag_ref[0:2]
    out_ref[base + 6 : base + 7] = group_rows(cross)
    out_ref[base + 7 : base + 8] = jnp.zeros_like(out_ref[base + 7 : base + 8])


def plane_join(length, own, other, lag, core_lag, rate):
    return pl.pallas_call(
        functools.partial(plane_kernel, length),
        out_shape=jax.ShapeDtypeStruct((2 * MODES + 8, own.shape[1]), F32),
        compiler_params=params(),
        name="plane_join",
    )(own, other, lag, core_lag, rate)


def add_row(rows, extra):
    return rows + jnp.where(row_iota(rows.shape) == 6, extra, 0.0)


def line_kernel(length, mask, final, own_ref, other_ref, rate_ref, out_ref):
    index = position()
    rate = rate_ref[:, quarter_of(index, own_ref.shape[1])]
    end, start, cross = join(
        own_ref[...],
        other_ref[...],
        bit_of(index, mask),
        jnp.exp(-rate * (mask * length)),
        jnp.exp(-rate),
    )
    rows = add_row(own_ref[2 * MODES :] + other_ref[2 * MODES :], group_rows(cross))
    if final:
        out_ref[:MODES] = jnp.where(bit_of(index, 2 * mask), start, end)
        out_ref[MODES:] = rows
    else:
        out_ref[:MODES] = end
        out_ref[MODES : 2 * MODES] = start
        out_ref[2 * MODES :] = rows


def line_join(length, mask, final, own, other, rate):
    count = MODES + 8 if final else 2 * MODES + 8
    return pl.pallas_call(
        functools.partial(line_kernel, length, mask, final),
        out_shape=jax.ShapeDtypeStruct((count, own.shape[1]), F32),
        compiler_params=params(),
        name="line_join",
    )(own, other, rate)


def turn_kernel(length, masks, own_ref, other_ref, *refs):
    levels = refs[: len(masks) - 1]
    chip_ref, chip_other_ref, rate_ref, keep_ref, send_ref = refs[len(masks) - 1 :]
    index = position()
    rate = rate_ref[:, quarter_of(index, own_ref.shape[1])]
    own, other = own_ref[:MODES], other_ref[:MODES]
    late = bit_of(index, masks[-1])
    cross = own * other * jnp.exp(-rate)
    rows = add_row(own_ref[MODES:] + other_ref[MODES:], group_rows(cross))
    before = jnp.where(late, other, 0.0)
    after = jnp.where(late, 0.0, other)
    for mask, level in reversed(list(zip(masks[:-1], levels))):
        late = bit_of(index, mask)
        power = jnp.exp(-rate * (mask * length))
        before, after = (
            jnp.where(late, level[:MODES] + power * before, before),
            jnp.where(late, after, level[MODES : 2 * MODES] + power * after),
        )
    late = bit_of(index, 2)
    power = jnp.exp(-rate * (2 * length))
    early_end = jnp.where(late, chip_other_ref[:MODES], chip_ref[:MODES])
    late_start = jnp.where(late, chip_ref[MODES:], chip_other_ref[MODES:])
    early, later = pass_down(early_end, late_start, before, after, power)
    keep_ref[:MODES] = jnp.where(late, later[0], early[0])
    keep_ref[MODES : 2 * MODES] = jnp.where(late, later[1], early[1])
    keep_ref[2 * MODES :] = rows
    send_ref[:MODES] = jnp.where(late, early[0], later[0])
    send_ref[MODES : 2 * MODES] = jnp.where(late, early[1], later[1])
    send_ref[2 * MODES :] = rows


def turn(length, masks, own, other, levels, chip, chip_other, rate):
    shape = jax.ShapeDtypeStruct((2 * MODES + 8, own.shape[1]), F32)
    return pl.pallas_call(
        functools.partial(turn_kernel, length, masks),
        out_shape=[shape, shape],
        compiler_params=params(),
        name="turn",
    )(own, other, *levels, chip, chip_other, rate)


def chip_kernel(length, own_ref, other_ref, core_ref, core_other_ref, rate_ref, keep_ref, send_ref):
    index = position()
    quarter = own_ref.shape[1]
    half = 2 * quarter
    rate = rate_ref[:, pl.ds(pl.multiple_of((index & 1) * half, half), half)]
    power = jnp.exp(-rate * length)
    second = bit_of(index, 2)
    own, other = own_ref[...], other_ref[...]
    left = jnp.where(second, other, own)
    right = jnp.where(second, own, other)
    around = jnp.concatenate([left[: 2 * MODES], right[: 2 * MODES]], axis=1)
    before, after = around[:MODES], around[MODES:]
    late = bit_of(index, 1)
    early_end = jnp.where(late, core_other_ref[:MODES], core_ref[:MODES])
    late_start = jnp.where(late, core_ref[MODES:], core_other_ref[MODES:])
    early, later = pass_down(early_end, late_start, before, after, power)
    base = 2 * MODES
    rows = own[base:] + other[base:]
    cross = jnp.concatenate(
        [rows[4:5] + left[base + 6 : base + 7], rows[5:6] + right[base + 6 : base + 7]], axis=1
    )
    sums = jnp.concatenate(
        [
            jnp.concatenate([rows[0:1], rows[1:2]], axis=1),
            jnp.concatenate([rows[2:3], rows[3:4]], axis=1),
            cross,
            jnp.zeros((5, half), F32),
        ],
        axis=0,
    )
    keep_ref[:MODES] = jnp.where(late, later[0], early[0])
    keep_ref[MODES:base] = jnp.where(late, later[1], early[1])
    keep_ref[base:] = sums
    send_ref[:MODES] = jnp.where(late, early[0], later[0])
    send_ref[MODES:base] = jnp.where(late, early[1], later[1])
    send_ref[base:] = sums


def chip_split(length, own, other, core, core_other, rate):
    shape = jax.ShapeDtypeStruct((2 * MODES + 8, 2 * own.shape[1]), F32)
    return pl.pallas_call(
        functools.partial(chip_kernel, length),
        out_shape=[shape, shape],
        compiler_params=params(),
        name="chip_split",
    )(own, other, core, core_other, rate)


def spread(state):
    same = lane_iota((LANES, LANES)) // PER == row_iota((LANES, LANES)) // MODES
    return jnp.where(same, jnp.concatenate([state] * PACK, axis=0), 0.0)


def carried(high_ref, low_ref, lanes, state):
    high, low = split(spread(state))
    table = high_ref[:, lanes]
    return jnp.dot(
        jnp.concatenate([table, table, low_ref[:, lanes]], axis=1),
        jnp.concatenate([high, low, high], axis=0),
        preferred_element_type=F32,
    )


def outputs_kernel(
    scale,
    own_ref,
    other_ref,
    decay_ref,
    q_ref,
    k_ref,
    v_ref,
    c_ref,
    fore_ref,
    back_ref,
    fh_ref,
    fl_ref,
    bh_ref,
    bl_ref,
    out_ref,
    query_ref,
    key_ref,
    value_ref,
    grad_ref,
):
    step = pl.program_id(0)
    steps = pl.num_programs(0)
    index = position()
    width = q_ref.shape[1]
    late = bit_of(index, 1)
    mine = (step >= steps // 2) == late
    place = pl.ds(pl.multiple_of((step % (steps // 2)) * width, width), width)
    around = jnp.where(mine, own_ref[: 2 * MODES, place], other_ref[: 2 * MODES, place])
    for block in range(width // LANES):
        lanes = slice(block * LANES, (block + 1) * LANES)
        mixed = fore_ref[:, lanes] + carried(fh_ref, fl_ref, lanes, around[:MODES, lanes])
        out_ref[:, lanes] = (q_ref[:, lanes].astype(F32) * mixed).astype(BF16)
        query_ref[:, lanes] = (c_ref[:, lanes].astype(F32) * mixed).astype(BF16)
        grad = back_ref[:, lanes] + carried(bh_ref, bl_ref, lanes, around[MODES:, lanes])
        key_ref[:, lanes] = (grad * v_ref[:, lanes].astype(F32)).astype(BF16)
        value_ref[:, lanes] = (grad * k_ref[:, lanes].astype(F32)).astype(BF16)

    @pl.when(step == 0)
    def _():
        base = 2 * MODES
        half = own_ref.shape[1]
        own, other = own_ref[base:], other_ref[base:]
        lags = own[0:2] + other[0:2]
        first = jnp.where(late, other[2:3], own[2:3])
        second = jnp.where(late, own[2:3], other[2:3])
        rows = [lags[0:1] + first, lags[1:2] + second]
        blocks = half // LANES
        for i in range(2 * blocks):
            row = rows[i // blocks][:, (i % blocks) * LANES : (i % blocks + 1) * LANES]
            spun = jnp.broadcast_to(row, (PACK, LANES))
            for bit in (1, 2, 4):
                turned = pltpu.roll(spun, LANES - bit * MODES, 1)
                spun = jnp.where((row_iota(spun.shape) & bit) != 0, turned, spun)
            groups = slice(i * PACK, (i + 1) * PACK)
            rate = decay_ref[groups, :]
            grad_ref[groups, :] = spun[:, :MODES] * jnp.sqrt(2.0 * rate / MODES) * scale


def outputs(scale, own, other, decay, q, k, v, c, fore, back, table):
    length, total = q.shape
    steps = 4
    width = total // steps
    stream = pl.BlockSpec((length, width), lambda i: (0, i))
    whole = pl.BlockSpec(own.shape, lambda i: (0, 0))
    small = pl.BlockSpec(decay.shape, lambda i: (0, 0))
    wide = jax.ShapeDtypeStruct((length, total), BF16)
    return pl.pallas_call(
        functools.partial(outputs_kernel, scale),
        grid=(steps,),
        in_specs=[whole, whole, small] + [stream] * 10,
        out_specs=[stream] * 4 + [small],
        out_shape=[wide] * 4 + [jax.ShapeDtypeStruct(decay.shape, F32)],
        compiler_params=params(),
        name="outputs",
    )(own, other, decay, q, k, v, c, fore, back, *table)


def per_device(query, key, value, cotangent, decay, residue):
    length = query.shape[0]
    count = lax.axis_size("seq")
    masks = [1 << i for i in range(2, count.bit_length() - 1)]

    def swap(array, mask):
        return lax.ppermute(array, "seq", [(i, i ^ mask) for i in range(count)])

    core_send, core, rate = states(key, value, query, cotangent, decay)
    core_other = swap(core_send, 1)
    weight, *table = tables(decay, residue, length)
    chip_send, chip, core_lag = core_join(length, core, core_other, rate)
    chip_other = swap(chip_send, 2)
    lag = lag_part(key, value, query, cotangent, rate)
    message = plane_join(length, chip, chip_other, lag, core_lag, rate)
    levels = []
    for mask in masks[:-1]:
        levels.append(swap(message, mask))
        message = line_join(length, mask, mask == masks[-2], message, levels[-1], rate)
    fore = scan_part(key, value, rate, weight, False)
    top = swap(message, masks[-1])
    keep, send = turn(length, masks, message, top, levels, chip, chip_other, rate)
    back = scan_part(query, cotangent, rate, weight, True)
    arrived = swap(send, 2)
    own, send = chip_split(length, keep, arrived, core, core_other, rate)
    other = swap(send, 1)
    scale = 1.0 / math.sqrt(length * count)
    return outputs(scale, own, other, decay, query, key, value, cotangent, fore, back, table)


def solution(mesh):
    rows = P(("grp", "seq"), None)
    return jax.shard_map(
        per_device,
        mesh=mesh,
        in_specs=(rows, rows, rows, rows, P(), P()),
        out_specs=(rows, rows, rows, rows, P("grp", None)),
        check_vma=False,
    )
```

```python
import functools
import math

import jax
import jax.numpy as jnp
from jax import lax
from jax.experimental import pallas as pl
from jax.experimental.pallas import tpu as pltpu
from jax.sharding import PartitionSpec as P

PER = 16
MODES = 16
LANES = 128
PACK = LANES // PER
F32 = jnp.float32
BF16 = jnp.bfloat16


def lane_iota(shape):
    return lax.broadcasted_iota(jnp.int32, shape, 1)


def row_iota(shape):
    return lax.broadcasted_iota(jnp.int32, shape, 0)


def split(value):
    high = value.astype(BF16)
    return high, (value - high.astype(F32)).astype(BF16)


def lanes_of(block):
    return slice(block * LANES, (block + 1) * LANES)


def rows_of(block):
    return slice(block * MODES, (block + 1) * MODES)


def dot3(left, right):
    left_high, left_low = split(left)
    right_high, right_low = split(right)
    return jnp.dot(
        jnp.concatenate([left_high, left_high, left_low], axis=1),
        jnp.concatenate([right_high, right_low, right_high], axis=0),
        preferred_element_type=F32,
    )


def own_group(stack):
    group = lane_iota((MODES, LANES)) // PER
    total = stack[rows_of(0)]
    for g in range(1, PACK):
        total = jnp.where(group == g, stack[rows_of(g)], total)
    return total


def columns(by_filter, first):
    return jnp.concatenate(
        [
            jnp.broadcast_to(by_filter[:, g : g + 1], (MODES, LANES))
            for g in range(first, first + PACK)
        ],
        axis=0,
    )


def filter_sums(stack, first):
    high, low = split(stack)
    spot = lane_iota((LANES, LANES)) % PACK == row_iota((LANES, LANES)) // PER
    spot = spot.astype(F32).astype(BF16)
    sums = jnp.dot(
        jnp.concatenate([high, low], axis=1),
        jnp.concatenate([spot, spot], axis=0),
        preferred_element_type=F32,
    )
    block = lane_iota((MODES, LANES)) // PACK - first
    total = jnp.zeros((MODES, LANES), F32)
    for i in range(stack.shape[0] // MODES):
        total = total + jnp.where(block == i, sums[rows_of(i)], 0.0)
    return total


def bit_of(index, mask):
    return (index & mask) != 0


def call(kernel, name, outs, *operands, scratch=(), outs_in=None, ins_in=None):
    ins_in = ins_in or [pltpu.VMEM] * len(operands)
    outs_in = outs_in or [pltpu.VMEM] * len(outs)
    return pl.pallas_call(
        kernel,
        in_specs=[pl.BlockSpec(memory_space=space) for space in ins_in],
        out_specs=[pl.BlockSpec(memory_space=space) for space in outs_in],
        out_shape=[jax.ShapeDtypeStruct(shape, dtype) for shape, dtype in outs],
        scratch_shapes=list(scratch),
        compiler_params=pltpu.CompilerParams(vmem_limit_bytes=16 << 20),
        name=name,
    )(*operands)


CHUNKS = 4


def states_kernel(
    k_hbm,
    v_hbm,
    q_hbm,
    c_hbm,
    decay_hbm,
    send_ref,
    keep_ref,
    rate_ref,
    gated_ref,
    upstream_ref,
    k_ref,
    v_ref,
    q_ref,
    c_ref,
    decay_ref,
    sems,
    decay_sem,
):
    length, total = gated_ref.shape
    width = total // CHUNKS
    core = lax.axis_index("seq") & 1
    copies = [
        [
            pltpu.make_async_copy(
                source.at[:, pl.ds(i * width, width)],
                target.at[:, pl.ds(i * width, width)],
                sems.at[n, i],
            )
            for n, (source, target) in enumerate(
                [(k_hbm, k_ref), (v_hbm, v_ref), (q_hbm, q_ref), (c_hbm, c_ref)]
            )
        ]
        for i in range(CHUNKS)
    ]
    decay_copy = pltpu.make_async_copy(decay_hbm, decay_ref, decay_sem)
    decay_copy.start()
    for chunk in copies:
        for copy in chunk:
            copy.start()
    decay_copy.wait()
    time = lane_iota((LANES, length)).astype(F32)
    decay = decay_ref[...]
    blocks = width // LANES
    for i, chunk in enumerate(copies):
        rates = [columns(decay, (i * blocks + n) * PACK) for n in range(blocks)]
        for copy in chunk:
            copy.wait()
        ends = []
        starts = []
        for n in range(blocks):
            block = i * blocks + n
            lanes = lanes_of(block)
            gated = k_ref[:, lanes].astype(F32) * v_ref[:, lanes].astype(F32)
            upstream = q_ref[:, lanes].astype(F32) * c_ref[:, lanes].astype(F32)
            gated_ref[:, lanes] = gated
            upstream_ref[:, lanes] = upstream
            rate = rates[n]
            rate_ref[rows_of(block)] = own_group(rate)
            ends.append(own_group(dot3(jnp.exp(-rate * (length - 1.0 - time)), gated)))
            starts.append(own_group(dot3(jnp.exp(-rate * time), upstream)))
        half = i // (CHUNKS // 2)
        tall = blocks * MODES
        base = (i % (CHUNKS // 2)) * tall
        offset = total // 2 // LANES * MODES

        def store(ref, ends=ends, starts=starts, base=base, tall=tall, offset=offset):
            ref[base : base + tall] = jnp.concatenate(ends, axis=0)
            ref[offset + base : offset + base + tall] = jnp.concatenate(starts, axis=0)

        pl.when(core == half)(functools.partial(store, keep_ref))
        pl.when(core != half)(functools.partial(store, send_ref))


def states(k, v, q, c, decay):
    length, total = k.shape
    rows = total // LANES * MODES
    stream = ((length, total), k.dtype)
    wide = ((length, total), F32)
    stack = ((rows, LANES), F32)
    arrays = [pltpu.with_memory_space_constraint(x, pltpu.HBM) for x in (k, v, q, c, decay)]
    return call(
        states_kernel,
        "states",
        [stack, stack, stack, wide, wide] + [stream] * 4,
        *arrays,
        scratch=[
            pltpu.VMEM(decay.shape, F32),
            pltpu.SemaphoreType.DMA((4, CHUNKS)),
            pltpu.SemaphoreType.DMA,
        ],
        ins_in=[pltpu.HBM] * 5,
    )


def tables_kernel(decay_ref, residue_ref, rate_ref, weight_ref, fh_ref, fl_ref, bh_ref, bl_ref):
    length, total = fh_ref.shape
    weights = residue_ref[...] * jnp.sqrt(2.0 * decay_ref[...] / MODES)
    pick = lane_iota((MODES, LANES)) % MODES == row_iota((MODES, LANES))
    time = row_iota((MODES, LANES)).astype(F32)

    def across(stack):
        return jnp.sum(jnp.where(pick, stack, 0.0), axis=0, keepdims=True)

    for block in range(total // LANES):
        lanes = lanes_of(block)
        weight = own_group(columns(weights, block * PACK))
        weight_ref[rows_of(block)] = weight
        rate = jnp.broadcast_to(across(rate_ref[rows_of(block)]), (MODES, LANES))
        weight = jnp.broadcast_to(across(weight), (MODES, LANES))
        step = jnp.exp(-rate * MODES)
        fore = weight * jnp.exp(-rate * (time + 1.0))
        back = weight * jnp.exp(-rate * (MODES - time))
        for i in range(length // MODES):
            rows = rows_of(i)
            fh_ref[rows, lanes], fl_ref[rows, lanes] = split(fore)
            rows = rows_of(length // MODES - 1 - i)
            bh_ref[rows, lanes], bl_ref[rows, lanes] = split(back)
            fore = fore * step
            back = back * step


def tables(decay, residue, rate, length):
    total = rate.shape[0] // MODES * LANES
    return call(
        tables_kernel,
        "tables",
        [(rate.shape, F32)] + [((length, total), BF16)] * 4,
        decay,
        residue,
        rate,
    )


GROUP = 4


def lag_kernel(first, count, gated_ref, upstream_ref, rate_ref, out_ref):
    length = gated_ref.shape[0]
    out = jnp.zeros((MODES, LANES), F32)
    for start in range(first, first + count, GROUP):
        blocks = range(start, start + GROUP)
        decays = [jnp.exp(-rate_ref[rows_of(block)]) for block in blocks]

        def eight(i, carry, blocks=blocks, decays=decays):
            states, totals = list(carry[0]), list(carry[1])
            base = pl.multiple_of(i * 8, 8)
            xs = [gated_ref[pl.ds(base, 8), lanes_of(block)] for block in blocks]
            us = [upstream_ref[pl.ds(base, 8), lanes_of(block)] for block in blocks]
            for j in range(8):
                for n in range(GROUP):
                    x = jnp.broadcast_to(xs[n][j : j + 1], (MODES, LANES))
                    u = jnp.broadcast_to(us[n][j : j + 1], (MODES, LANES))
                    states[n] = states[n] * decays[n] + x
                    totals[n] = totals[n] + states[n] * u
            return tuple(states), tuple(totals)

        zeros = (jnp.zeros((MODES, LANES), F32),) * GROUP
        _, totals = lax.fori_loop(0, length // 8, eight, (zeros, zeros))
        out = out + filter_sums(jnp.concatenate(totals, axis=0), start)
    out_ref[...] = out


def lag_part(gated, upstream, rate, first, count):
    return call(
        functools.partial(lag_kernel, first, count),
        "lag_part",
        [((MODES, LANES), F32)],
        gated,
        upstream,
        rate,
    )[0]


def fold(first, second, shift, row):
    low = (row & shift) == 0
    kept = jnp.where(low, first, second)
    moved = jnp.where(low, second, first)
    return kept + pltpu.roll(moved, shift, 0)


def scan_kernel(reverse, first, count, in_ref, rate_ref, weight_ref, out_ref):
    length = in_ref.shape[0]
    row = row_iota((8, LANES))
    for start in range(first, first + count, GROUP):
        blocks = range(start, start + GROUP)
        decays = [jnp.exp(-rate_ref[rows_of(block)]) for block in blocks]
        weights = [weight_ref[rows_of(block)] for block in blocks]

        def eight(i, carry, blocks=blocks, decays=decays, weights=weights):
            states = list(carry)
            at = length // 8 - 1 - i if reverse else i
            base = pl.multiple_of(at * 8, 8)
            rows = [in_ref[pl.ds(base, 8), lanes_of(block)] for block in blocks]
            parts = [[None] * 8 for _ in blocks]
            for j in reversed(range(8)) if reverse else range(8):
                for n in range(GROUP):
                    x = jnp.broadcast_to(rows[n][j : j + 1], (MODES, LANES))
                    states[n] = states[n] * decays[n] + x
                    product = states[n] * weights[n]
                    parts[n][j] = product[:8] + product[8:]
            for n, block in enumerate(blocks):
                part = parts[n]
                four = [fold(part[2 * j], part[2 * j + 1], 1, row) for j in range(4)]
                two = [fold(four[2 * j], four[2 * j + 1], 2, row) for j in range(2)]
                place = lanes_of(block - first)
                out_ref[pl.ds(base, 8), place] = fold(two[0], two[1], 4, row)
            return tuple(states)

        zeros = (jnp.zeros((MODES, LANES), F32),) * GROUP
        lax.fori_loop(0, length // 8, eight, zeros)


def scan_part(values, rate, weight, reverse, first, count):
    return call(
        functools.partial(scan_kernel, reverse, first, count),
        "scan_back" if reverse else "scan_fore",
        [((values.shape[0], count * LANES), F32)],
        values,
        rate,
        weight,
    )[0]


def join(own, other, late, power, step_decay):
    half = power.shape[0]
    own_end, own_start = own[:half], own[half : 2 * half]
    other_end, other_start = other[:half], other[half : 2 * half]
    early_end = jnp.where(late, other_end, own_end)
    late_end = jnp.where(late, own_end, other_end)
    early_start = jnp.where(late, other_start, own_start)
    late_start = jnp.where(late, own_start, other_start)
    end = late_end + power * early_end
    start = early_start + power * late_start
    return end, start, early_end * late_start * step_decay


def pass_down(first, second, before, after, power):
    early = (before, second + power * after)
    late = (first + power * before, after)
    return early, late


def quarter_start(index, rows):
    return pl.multiple_of(((index & 1) * 2 + ((index >> 1) & 1)) * rows, rows)


def core_kernel(length, own_ref, other_ref, rate_ref, send_ref, keep_ref, sums_ref):
    index = lax.axis_index("seq")
    half = own_ref.shape[0] // 2
    quarter = half // 2
    at = pl.multiple_of((index & 1) * half, half)
    rate = rate_ref[pl.ds(at, half)]
    end, start, cross = join(
        own_ref[...],
        other_ref[...],
        bit_of(index, 1),
        jnp.exp(-rate * length),
        jnp.exp(-rate),
    )
    second = bit_of(index, 2)
    keep_ref[:quarter] = jnp.where(second, end[quarter:], end[:quarter])
    keep_ref[quarter:] = jnp.where(second, start[quarter:], start[:quarter])
    send_ref[:quarter] = jnp.where(second, end[:quarter], end[quarter:])
    send_ref[quarter:] = jnp.where(second, start[:quarter], start[quarter:])
    sums_ref[...] = filter_sums(cross, at // MODES)


def core_join(length, own, other, rate):
    half = ((own.shape[0] // 2, LANES), F32)
    return call(
        functools.partial(core_kernel, length),
        "core_join",
        [half, half, ((MODES, LANES), F32)],
        own,
        other,
        rate,
    )


def plane_kernel(length, own_ref, other_ref, *refs):
    *sums_refs, rate_ref, out_ref = refs
    index = lax.axis_index("seq")
    quarter = own_ref.shape[0] // 2
    at = quarter_start(index, quarter)
    rate = rate_ref[pl.ds(at, quarter)]
    end, start, cross = join(
        own_ref[...],
        other_ref[...],
        bit_of(index, 2),
        jnp.exp(-rate * (2 * length)),
        jnp.exp(-rate),
    )
    out_ref[:quarter] = end
    out_ref[quarter : 2 * quarter] = start
    sums = filter_sums(cross, at // MODES)
    for ref in sums_refs:
        sums = sums + ref[...]
    out_ref[2 * quarter :] = sums


def plane_join(length, own, other, sums, rate):
    return call(
        functools.partial(plane_kernel, length),
        "plane_join",
        [((own.shape[0] + MODES, LANES), F32)],
        own,
        other,
        *sums,
        rate,
    )[0]


def line_kernel(length, mask, final, own_ref, other_ref, rate_ref, out_ref):
    index = lax.axis_index("seq")
    quarter = (own_ref.shape[0] - MODES) // 2
    at = quarter_start(index, quarter)
    rate = rate_ref[pl.ds(at, quarter)]
    end, start, cross = join(
        own_ref[...],
        other_ref[...],
        bit_of(index, mask),
        jnp.exp(-rate * (mask * length)),
        jnp.exp(-rate),
    )
    sums = own_ref[2 * quarter :] + other_ref[2 * quarter :] + filter_sums(cross, at // MODES)
    if final:
        out_ref[:quarter] = jnp.where(bit_of(index, 2 * mask), start, end)
        out_ref[quarter:] = sums
    else:
        out_ref[:quarter] = end
        out_ref[quarter : 2 * quarter] = start
        out_ref[2 * quarter :] = sums


def line_join(length, mask, final, own, other, rate):
    quarter = (own.shape[0] - MODES) // 2
    count = (quarter if final else 2 * quarter) + MODES
    return call(
        functools.partial(line_kernel, length, mask, final),
        "line_join",
        [((count, LANES), F32)],
        own,
        other,
        rate,
    )[0]


def turn_kernel(length, masks, own_ref, other_ref, *refs):
    levels = refs[: len(masks) - 1]
    chip_ref, chip_other_ref, rate_ref, keep_ref, send_ref = refs[len(masks) - 1 :]
    index = lax.axis_index("seq")
    quarter = own_ref.shape[0] - MODES
    at = quarter_start(index, quarter)
    rate = rate_ref[pl.ds(at, quarter)]
    own, other = own_ref[:quarter], other_ref[:quarter]
    late = bit_of(index, masks[-1])
    cross = own * other * jnp.exp(-rate)
    sums = own_ref[quarter:] + other_ref[quarter:] + filter_sums(cross, at // MODES)
    before = jnp.where(late, other, 0.0)
    after = jnp.where(late, 0.0, other)
    for mask, level in reversed(list(zip(masks[:-1], levels))):
        late = bit_of(index, mask)
        power = jnp.exp(-rate * (mask * length))
        before, after = (
            jnp.where(late, level[:quarter] + power * before, before),
            jnp.where(late, after, level[quarter : 2 * quarter] + power * after),
        )
    late = bit_of(index, 2)
    power = jnp.exp(-rate * (2 * length))
    early_end = jnp.where(late, chip_other_ref[:quarter], chip_ref[:quarter])
    late_start = jnp.where(late, chip_ref[quarter:], chip_other_ref[quarter:])
    early, later = pass_down(early_end, late_start, before, after, power)
    keep_ref[:quarter] = jnp.where(late, later[0], early[0])
    keep_ref[quarter : 2 * quarter] = jnp.where(late, later[1], early[1])
    keep_ref[2 * quarter :] = sums
    send_ref[:quarter] = jnp.where(late, early[0], later[0])
    send_ref[quarter : 2 * quarter] = jnp.where(late, early[1], later[1])
    send_ref[2 * quarter :] = sums


def turn(length, masks, own, other, levels, chip, chip_other, rate):
    shape = ((chip.shape[0] + MODES, LANES), F32)
    return call(
        functools.partial(turn_kernel, length, masks),
        "turn",
        [shape, shape],
        own,
        other,
        *levels,
        chip,
        chip_other,
        rate,
    )


def chip_kernel(length, own_ref, other_ref, core_ref, core_other_ref, rate_ref, keep_ref, send_ref):
    index = lax.axis_index("seq")
    quarter = (own_ref.shape[0] - MODES) // 2
    half = 2 * quarter
    rate = rate_ref[pl.ds(pl.multiple_of((index & 1) * half, half), half)]
    power = jnp.exp(-rate * length)
    second = bit_of(index, 2)
    own, other = own_ref[:half], other_ref[:half]
    left = jnp.where(second, other, own)
    right = jnp.where(second, own, other)
    before = jnp.concatenate([left[:quarter], right[:quarter]], axis=0)
    after = jnp.concatenate([left[quarter:], right[quarter:]], axis=0)
    late = bit_of(index, 1)
    early_end = jnp.where(late, core_other_ref[:half], core_ref[:half])
    late_start = jnp.where(late, core_ref[half:], core_other_ref[half:])
    early, later = pass_down(early_end, late_start, before, after, power)
    sums = own_ref[half:] + other_ref[half:]
    keep_ref[:half] = jnp.where(late, later[0], early[0])
    keep_ref[half : 2 * half] = jnp.where(late, later[1], early[1])
    keep_ref[2 * half :] = sums
    send_ref[:half] = jnp.where(late, early[0], later[0])
    send_ref[half : 2 * half] = jnp.where(late, early[1], later[1])
    send_ref[2 * half :] = sums


def chip_split(length, own, other, core, core_other, rate):
    shape = ((core.shape[0] + MODES, LANES), F32)
    return call(
        functools.partial(chip_kernel, length),
        "chip_split",
        [shape, shape],
        own,
        other,
        core,
        core_other,
        rate,
    )


def spread(state):
    same = lane_iota((LANES, LANES)) // PER == row_iota((LANES, LANES)) // MODES
    return jnp.where(same, jnp.concatenate([state] * PACK, axis=0), 0.0)


def carried(high_ref, low_ref, lanes, state):
    high, low = split(spread(state))
    table = high_ref[:, lanes]
    return jnp.dot(
        jnp.concatenate([table, table, low_ref[:, lanes]], axis=1),
        jnp.concatenate([high, low, high], axis=0),
        preferred_element_type=F32,
    )


OUT_CHUNKS = 8


def outputs_kernel(scale, fores, backs, *refs):
    own_ref, other_ref, decay_ref, q_ref, k_ref, v_ref, c_ref = refs[:7]
    fore_refs = refs[7 : 7 + fores]
    back_refs = refs[7 + fores : 7 + fores + backs]
    fh_ref, fl_ref, bh_ref, bl_ref = refs[7 + fores + backs : 11 + fores + backs]
    out_hbm, query_hbm, key_hbm, value_hbm, grad_ref = refs[11 + fores + backs : 16 + fores + backs]
    out_ref, query_ref, key_ref, value_ref, sems = refs[16 + fores + backs :]
    core = lax.axis_index("seq") & 1
    length, total = q_ref.shape
    blocks = total // LANES
    half = (own_ref.shape[0] - MODES) // 2

    def local(pieces, block):
        each = pieces[0].shape[1] // LANES
        for piece in pieces:
            each = piece.shape[1] // LANES
            if block < each:
                return piece[:, lanes_of(block)]
            block -= each

    copies = []
    per_chunk = blocks // OUT_CHUNKS
    for chunk in range(OUT_CHUNKS):
        for block in range(chunk * per_chunk, (chunk + 1) * per_chunk):
            lanes = lanes_of(block)
            mine = core == block // (blocks // 2)
            at = (block % (blocks // 2)) * MODES
            ends = slice(at, at + MODES)
            starts = slice(half + at, half + at + MODES)
            before = jnp.where(mine, own_ref[ends], other_ref[ends])
            after = jnp.where(mine, own_ref[starts], other_ref[starts])
            mixed = local(fore_refs, block) + carried(fh_ref, fl_ref, lanes, before)
            out_ref[:, lanes] = (q_ref[:, lanes].astype(F32) * mixed).astype(BF16)
            query_ref[:, lanes] = (c_ref[:, lanes].astype(F32) * mixed).astype(BF16)
            grad = local(back_refs, block) + carried(bh_ref, bl_ref, lanes, after)
            key_ref[:, lanes] = (grad * v_ref[:, lanes].astype(F32)).astype(BF16)
            value_ref[:, lanes] = (grad * k_ref[:, lanes].astype(F32)).astype(BF16)
        place = pl.ds(chunk * per_chunk * LANES, per_chunk * LANES)
        for n, (source, target) in enumerate(
            [(out_ref, out_hbm), (query_ref, query_hbm), (key_ref, key_hbm), (value_ref, value_hbm)]
        ):
            copy = pltpu.make_async_copy(source.at[:, place], target.at[:, place], sems.at[n, chunk])
            copy.start()
            copies.append(copy)
    sums = own_ref[2 * half :] + other_ref[2 * half :]
    grad_ref[...] = sums * jnp.sqrt(2.0 * decay_ref[...] / MODES) * scale
    for copy in copies:
        copy.wait()


def outputs(scale, own, other, decay, q, k, v, c, fore, back, table):
    length, total = q.shape
    wide = ((length, total), BF16)
    return call(
        functools.partial(outputs_kernel, scale, len(fore), len(back)),
        "outputs",
        [wide] * 4 + [(decay.shape, F32)],
        own,
        other,
        decay,
        q,
        k,
        v,
        c,
        *fore,
        *back,
        *table,
        scratch=[pltpu.VMEM((length, total), BF16)] * 4 + [pltpu.SemaphoreType.DMA((4, OUT_CHUNKS))],
        outs_in=[pltpu.HBM] * 4 + [pltpu.VMEM],
    )


def tie(*values):
    return lax.optimization_barrier(values)


def per_device(query, key, value, cotangent, decay, residue):
    length, total = query.shape
    blocks = total // LANES
    count = lax.axis_size("seq")
    masks = [1 << i for i in range(2, count.bit_length() - 1)]
    decay, residue = decay.T, residue.T

    def swap(array, mask):
        return lax.ppermute(array, "seq", [(i, i ^ mask) for i in range(count)])

    core_send, core, rate, gated, upstream, k, v, q, c = states(key, value, query, cotangent, decay)
    core_other = swap(core_send, 1)
    quarter = blocks // 4
    lag_first = lag_part(gated, upstream, rate, 0, quarter)
    core_other, lag_first = tie(core_other, lag_first)
    chip_send, chip, core_sums = core_join(length, core, core_other, rate)
    chip_send, gated, upstream = tie(chip_send, gated, upstream)
    chip_other = swap(chip_send, 2)
    lag_rest = lag_part(gated, upstream, rate, quarter, blocks - quarter)
    message = plane_join(length, chip, chip_other, [core_sums, lag_first, lag_rest], rate)
    message, gated, upstream, rate = tie(message, gated, upstream, rate)
    levels = []
    fore = []
    back = []
    for mask in masks[:-1]:
        levels.append(swap(message, mask))
        if mask == masks[0]:
            weight, *table = tables(decay, residue, rate, length)
            fore.append(scan_part(gated, rate, weight, False, 0, blocks // 2))
            levels[-1], fore[-1] = tie(levels[-1], fore[-1])
        message = line_join(length, mask, mask == masks[-2], message, levels[-1], rate)
    message, gated, upstream, rate = tie(message, gated, upstream, rate)
    top = swap(message, masks[-1])
    fore.append(scan_part(gated, rate, weight, False, blocks // 2, blocks // 2))
    top, fore[-1] = tie(top, fore[-1])
    keep, send = turn(length, masks, message, top, levels, chip, chip_other, rate)
    send, upstream, rate = tie(send, upstream, rate)
    arrived = swap(send, 2)
    back.append(scan_part(upstream, rate, weight, True, 0, blocks // 2))
    arrived, back[-1] = tie(arrived, back[-1])
    own, send = chip_split(length, keep, arrived, core, core_other, rate)
    send, upstream, rate = tie(send, upstream, rate)
    other = swap(send, 1)
    back.append(scan_part(upstream, rate, weight, True, blocks // 2, blocks // 2))
    scale = 1.0 / math.sqrt(length * count)
    *wide, grad = outputs(scale, own, other, decay, q, k, v, c, fore, back, table)
    return (*wide, grad.T)


def solution(mesh):
    rows = P(("grp", "seq"), None)
    return jax.shard_map(
        per_device,
        mesh=mesh,
        in_specs=(rows, rows, rows, rows, P(), P()),
        out_specs=(rows, rows, rows, rows, P("grp", None)),
        check_vma=False,
    )
```

```python
import functools
import math

import jax
import jax.numpy as jnp
from jax import lax
from jax.experimental import pallas as pl
from jax.experimental.pallas import tpu as pltpu
from jax.sharding import PartitionSpec as P

PER = 16
MODES = 16
LANES = 128
PACK = LANES // PER
F32 = jnp.float32
BF16 = jnp.bfloat16


def lane_iota(shape):
    return lax.broadcasted_iota(jnp.int32, shape, 1)


def row_iota(shape):
    return lax.broadcasted_iota(jnp.int32, shape, 0)


def split(value):
    high = value.astype(BF16)
    return high, (value - high.astype(F32)).astype(BF16)


def lanes_of(block):
    return slice(block * LANES, (block + 1) * LANES)


def rows_of(block):
    return slice(block * MODES, (block + 1) * MODES)


def dot3(left, right):
    left_high, left_low = split(left)
    right_high, right_low = split(right)
    return jnp.dot(
        jnp.concatenate([left_high, left_high, left_low], axis=1),
        jnp.concatenate([right_high, right_low, right_high], axis=0),
        preferred_element_type=F32,
    )


def own_group(stack):
    group = lane_iota((MODES, LANES)) // PER
    total = stack[rows_of(0)]
    for g in range(1, PACK):
        total = jnp.where(group == g, stack[rows_of(g)], total)
    return total


def columns(by_filter, first):
    return jnp.concatenate(
        [
            jnp.broadcast_to(by_filter[:, g : g + 1], (MODES, LANES))
            for g in range(first, first + PACK)
        ],
        axis=0,
    )


def filter_sums(stack, first):
    high, low = split(stack)
    spot = lane_iota((LANES, LANES)) % PACK == row_iota((LANES, LANES)) // PER
    spot = spot.astype(F32).astype(BF16)
    sums = jnp.dot(
        jnp.concatenate([high, low], axis=1),
        jnp.concatenate([spot, spot], axis=0),
        preferred_element_type=F32,
    )
    block = lane_iota((MODES, LANES)) // PACK - first
    total = jnp.zeros((MODES, LANES), F32)
    for i in range(stack.shape[0] // MODES):
        total = total + jnp.where(block == i, sums[rows_of(i)], 0.0)
    return total


def bit_of(index, mask):
    return (index & mask) != 0


def kept_half(index):
    for shift in (8, 4, 2, 1):
        index = index ^ (index >> shift)
    return index & 1


def call(kernel, name, outs, *operands, scratch=(), outs_in=None, ins_in=None):
    ins_in = ins_in or [pltpu.VMEM] * len(operands)
    outs_in = outs_in or [pltpu.VMEM] * len(outs)
    return pl.pallas_call(
        kernel,
        in_specs=[pl.BlockSpec(memory_space=space) for space in ins_in],
        out_specs=[pl.BlockSpec(memory_space=space) for space in outs_in],
        out_shape=[jax.ShapeDtypeStruct(shape, dtype) for shape, dtype in outs],
        scratch_shapes=list(scratch),
        compiler_params=pltpu.CompilerParams(vmem_limit_bytes=16 << 20),
        name=name,
    )(*operands)


def of_half(by_filter, half):
    return jnp.where(half == 0, by_filter, pltpu.roll(by_filter, LANES // 2, 1))


def half_states(decay, k_ref, v_ref, q_ref, c_ref, state_ref, rate_ref, gated_ref, upstream_ref):
    length, width = gated_ref.shape
    time = lane_iota((LANES, length)).astype(F32)
    blocks = width // LANES
    for block in range(blocks):
        lanes = lanes_of(block)
        gated = k_ref[:, lanes].astype(F32) * v_ref[:, lanes].astype(F32)
        upstream = q_ref[:, lanes].astype(F32) * c_ref[:, lanes].astype(F32)
        gated_ref[:, lanes] = gated
        upstream_ref[:, lanes] = upstream
        rate = columns(decay, block * PACK)
        rate_ref[rows_of(block)] = own_group(rate)
        end = own_group(dot3(jnp.exp(-rate * (length - 1.0 - time)), gated))
        start = own_group(dot3(jnp.exp(-rate * time), upstream))
        state_ref[rows_of(block)] = end
        state_ref[rows_of(blocks + block)] = start


def send_states_kernel(*refs):
    sources, decay_hbm = refs[:4], refs[4]
    state_ref, rate_ref, gated_ref, upstream_ref, decay_ref = refs[5:10]
    sent, kept = refs[10:14], refs[14:18]
    sems, decay_sem = refs[18:]
    half = kept_half(lax.axis_index("seq"))
    width = gated_ref.shape[1]
    decay_copy = pltpu.make_async_copy(decay_hbm, decay_ref, decay_sem)
    decay_copy.start()
    copies = []
    for role, targets in enumerate([sent, kept]):
        at = pl.multiple_of((half if role else 1 - half) * width, width)
        for n in range(4):
            copy = pltpu.make_async_copy(
                sources[n].at[:, pl.ds(at, width)], targets[n], sems.at[role, n]
            )
            copy.start()
            copies.append(copy)
    decay_copy.wait()
    decay = of_half(decay_ref[...], 1 - half)
    for copy in copies[:4]:
        copy.wait()
    half_states(decay, *sent, state_ref, rate_ref, gated_ref, upstream_ref)
    for copy in copies[4:]:
        copy.wait()


def keep_states_kernel(decay_ref, *refs):
    decay = of_half(decay_ref[...], kept_half(lax.axis_index("seq")))
    half_states(decay, *refs)


def state_shapes(length, width):
    blocks = width // LANES
    return [
        ((2 * blocks * MODES, LANES), F32),
        ((blocks * MODES, LANES), F32),
        ((length, width), F32),
        ((length, width), F32),
    ]


def send_states(k, v, q, c, decay):
    length, total = k.shape
    arrays = [pltpu.with_memory_space_constraint(x, pltpu.HBM) for x in (k, v, q, c, decay)]
    outs = call(
        send_states_kernel,
        "send_states",
        state_shapes(length, total // 2)
        + [(decay.shape, F32)]
        + [((length, total // 2), k.dtype)] * 8,
        *arrays,
        scratch=[pltpu.SemaphoreType.DMA((2, 4)), pltpu.SemaphoreType.DMA],
        ins_in=[pltpu.HBM] * 5,
    )
    return outs[:4], outs[4], outs[5:9], outs[9:]


def keep_states(decay, streams):
    return call(
        keep_states_kernel, "keep_states", state_shapes(*streams[0].shape), decay, *streams
    )


def tables_kernel(keep, decay_ref, residue_ref, rate_ref, *refs):
    weight_ref, fh_ref, fl_ref, bh_ref, bl_ref = refs
    length, width = fh_ref.shape
    half = kept_half(lax.axis_index("seq"))
    weights = residue_ref[...] * jnp.sqrt(2.0 * decay_ref[...] / MODES)
    weights = of_half(weights, half if keep else 1 - half)
    pick = lane_iota((MODES, LANES)) % MODES == row_iota((MODES, LANES))
    time = row_iota((MODES, LANES)).astype(F32)

    def across(stack):
        return jnp.sum(jnp.where(pick, stack, 0.0), axis=0, keepdims=True)

    for block in range(width // LANES):
        lanes = lanes_of(block)
        weight = own_group(columns(weights, block * PACK))
        weight_ref[rows_of(block)] = weight
        rate = jnp.broadcast_to(across(rate_ref[rows_of(block)]), (MODES, LANES))
        weight = jnp.broadcast_to(across(weight), (MODES, LANES))
        step = jnp.exp(-rate * MODES)
        fore = weight * jnp.exp(-rate * (time + 1.0))
        back = weight * jnp.exp(-rate * (MODES - time))
        for i in range(length // MODES):
            rows = rows_of(i)
            fh_ref[rows, lanes], fl_ref[rows, lanes] = split(fore)
            rows = rows_of(length // MODES - 1 - i)
            bh_ref[rows, lanes], bl_ref[rows, lanes] = split(back)
            fore = fore * step
            back = back * step


def tables(keep, decay, residue, rate, length):
    width = rate.shape[0] // MODES * LANES
    return call(
        functools.partial(tables_kernel, keep),
        "tables",
        [(rate.shape, F32)] + [((length, width), BF16)] * 4,
        decay,
        residue,
        rate,
    )


GROUP = 4


def lag_kernel(keep, first, count, gated_ref, upstream_ref, rate_ref, out_ref):
    length, width = gated_ref.shape
    half = kept_half(lax.axis_index("seq"))
    offset = (half if keep else 1 - half) * (width // LANES)
    out = jnp.zeros((MODES, LANES), F32)
    for start in range(first, first + count, GROUP):
        blocks = range(start, start + GROUP)
        decays = [jnp.exp(-rate_ref[rows_of(block)]) for block in blocks]

        def eight(i, carry, blocks=blocks, decays=decays):
            states, totals = list(carry[0]), list(carry[1])
            base = pl.multiple_of(i * 8, 8)
            xs = [gated_ref[pl.ds(base, 8), lanes_of(block)] for block in blocks]
            us = [upstream_ref[pl.ds(base, 8), lanes_of(block)] for block in blocks]
            for j in range(8):
                for n in range(GROUP):
                    x = jnp.broadcast_to(xs[n][j : j + 1], (MODES, LANES))
                    u = jnp.broadcast_to(us[n][j : j + 1], (MODES, LANES))
                    states[n] = states[n] * decays[n] + x
                    totals[n] = totals[n] + states[n] * u
            return tuple(states), tuple(totals)

        zeros = (jnp.zeros((MODES, LANES), F32),) * GROUP
        _, totals = lax.fori_loop(0, length // 8, eight, (zeros, zeros))
        out = out + filter_sums(jnp.concatenate(totals, axis=0), offset + start)
    out_ref[...] = out


def lag_part(keep, gated, upstream, rate, first, count):
    return call(
        functools.partial(lag_kernel, keep, first, count),
        "lag_part",
        [((MODES, LANES), F32)],
        gated,
        upstream,
        rate,
    )[0]


def fold(first, second, shift, row):
    low = (row & shift) == 0
    kept = jnp.where(low, first, second)
    moved = jnp.where(low, second, first)
    return kept + pltpu.roll(moved, shift, 0)


def scan_kernel(tasks, *refs):
    row = row_iota((8, LANES))
    for n, (reverse, start) in enumerate(tasks):
        in_ref, rate_ref, weight_ref = refs[3 * n : 3 * n + 3]
        out_ref = refs[3 * len(tasks) + n]
        length = in_ref.shape[0]
        blocks = range(start, start + GROUP)
        decays = [jnp.exp(-rate_ref[rows_of(block)]) for block in blocks]
        weights = [weight_ref[rows_of(block)] for block in blocks]

        def eight(
            i,
            carry,
            reverse=reverse,
            blocks=blocks,
            decays=decays,
            weights=weights,
            in_ref=in_ref,
            out_ref=out_ref,
        ):
            states = list(carry)
            at = length // 8 - 1 - i if reverse else i
            base = pl.multiple_of(at * 8, 8)
            rows = [in_ref[pl.ds(base, 8), lanes_of(block)] for block in blocks]
            parts = [[None] * 8 for _ in blocks]
            for j in reversed(range(8)) if reverse else range(8):
                for n in range(GROUP):
                    x = jnp.broadcast_to(rows[n][j : j + 1], (MODES, LANES))
                    states[n] = states[n] * decays[n] + x
                    product = states[n] * weights[n]
                    parts[n][j] = product[:8] + product[8:]
            for n, block in enumerate(blocks):
                part = parts[n]
                four = [fold(part[2 * j], part[2 * j + 1], 1, row) for j in range(4)]
                two = [fold(four[2 * j], four[2 * j + 1], 2, row) for j in range(2)]
                place = lanes_of(n)
                out_ref[pl.ds(base, 8), place] = fold(two[0], two[1], 4, row)
            return tuple(states)

        zeros = (jnp.zeros((MODES, LANES), F32),) * GROUP
        lax.fori_loop(0, length // 8, eight, zeros)


def scan_part(tasks):
    operands = [x for task in tasks for x in task[:3]]
    return call(
        functools.partial(scan_kernel, [task[3:] for task in tasks]),
        "scan",
        [((tasks[0][0].shape[0], GROUP * LANES), F32)] * len(tasks),
        *operands,
    )


def join(own, other, late, power, step_decay):
    half = power.shape[0]
    own_end, own_start = own[:half], own[half : 2 * half]
    other_end, other_start = other[:half], other[half : 2 * half]
    early_end = jnp.where(late, other_end, own_end)
    late_end = jnp.where(late, own_end, other_end)
    early_start = jnp.where(late, other_start, own_start)
    late_start = jnp.where(late, own_start, other_start)
    end = late_end + power * early_end
    start = early_start + power * late_start
    return end, start, early_end * late_start * step_decay


def pass_down(first, second, before, after, power):
    early = (before, second + power * after)
    late = (first + power * before, after)
    return early, late


def quarter_of(index, ref):
    rows = ref.shape[0] // 2
    return pl.ds(pl.multiple_of(((index >> 1) & 1) * rows, rows), rows)


def first_block(index, rows):
    return (kept_half(index) * 2 + ((index >> 1) & 1)) * (rows // MODES)


def core_kernel(length, own_ref, other_ref, rate_ref, send_ref, keep_ref, sums_ref):
    index = lax.axis_index("seq")
    half = own_ref.shape[0] // 2
    quarter = half // 2
    rate = rate_ref[...]
    end, start, cross = join(
        own_ref[...],
        other_ref[...],
        bit_of(index, 1),
        jnp.exp(-rate * length),
        jnp.exp(-rate),
    )
    second = bit_of(index, 2)
    keep_ref[:quarter] = jnp.where(second, end[quarter:], end[:quarter])
    keep_ref[quarter:] = jnp.where(second, start[quarter:], start[:quarter])
    send_ref[:quarter] = jnp.where(second, end[:quarter], end[quarter:])
    send_ref[quarter:] = jnp.where(second, start[:quarter], start[quarter:])
    sums_ref[...] = filter_sums(cross, kept_half(index) * (half // MODES))


def core_join(length, own, other, rate):
    half = ((own.shape[0] // 2, LANES), F32)
    return call(
        functools.partial(core_kernel, length),
        "core_join",
        [half, half, ((MODES, LANES), F32)],
        own,
        other,
        rate,
    )


def plane_kernel(length, own_ref, other_ref, *refs):
    *sums_refs, rate_ref, out_ref = refs
    index = lax.axis_index("seq")
    quarter = own_ref.shape[0] // 2
    rate = rate_ref[quarter_of(index, rate_ref)]
    end, start, cross = join(
        own_ref[...],
        other_ref[...],
        bit_of(index, 2),
        jnp.exp(-rate * (2 * length)),
        jnp.exp(-rate),
    )
    out_ref[:quarter] = end
    out_ref[quarter : 2 * quarter] = start
    sums = filter_sums(cross, first_block(index, quarter))
    for ref in sums_refs:
        sums = sums + ref[...]
    out_ref[2 * quarter :] = sums


def plane_join(length, own, other, sums, rate):
    return call(
        functools.partial(plane_kernel, length),
        "plane_join",
        [((own.shape[0] + MODES, LANES), F32)],
        own,
        other,
        *sums,
        rate,
    )[0]


def line_kernel(length, mask, final, own_ref, other_ref, rate_ref, out_ref):
    index = lax.axis_index("seq")
    quarter = (own_ref.shape[0] - MODES) // 2
    rate = rate_ref[quarter_of(index, rate_ref)]
    end, start, cross = join(
        own_ref[...],
        other_ref[...],
        bit_of(index, mask),
        jnp.exp(-rate * (mask * length)),
        jnp.exp(-rate),
    )
    sums = own_ref[2 * quarter :] + other_ref[2 * quarter :] + filter_sums(cross, first_block(index, quarter))
    if final:
        out_ref[:quarter] = jnp.where(bit_of(index, 2 * mask), start, end)
        out_ref[quarter:] = sums
    else:
        out_ref[:quarter] = end
        out_ref[quarter : 2 * quarter] = start
        out_ref[2 * quarter :] = sums


def line_join(length, mask, final, own, other, rate):
    quarter = (own.shape[0] - MODES) // 2
    count = (quarter if final else 2 * quarter) + MODES
    return call(
        functools.partial(line_kernel, length, mask, final),
        "line_join",
        [((count, LANES), F32)],
        own,
        other,
        rate,
    )[0]


def turn_kernel(length, masks, own_ref, other_ref, *refs):
    levels = refs[: len(masks) - 1]
    chip_ref, chip_other_ref, rate_ref, keep_ref, send_ref = refs[len(masks) - 1 :]
    index = lax.axis_index("seq")
    quarter = own_ref.shape[0] - MODES
    rate = rate_ref[quarter_of(index, rate_ref)]
    own, other = own_ref[:quarter], other_ref[:quarter]
    late = bit_of(index, masks[-1])
    cross = own * other * jnp.exp(-rate)
    sums = own_ref[quarter:] + other_ref[quarter:] + filter_sums(cross, first_block(index, quarter))
    before = jnp.where(late, other, 0.0)
    after = jnp.where(late, 0.0, other)
    for mask, level in reversed(list(zip(masks[:-1], levels))):
        late = bit_of(index, mask)
        power = jnp.exp(-rate * (mask * length))
        before, after = (
            jnp.where(late, level[:quarter] + power * before, before),
            jnp.where(late, after, level[quarter : 2 * quarter] + power * after),
        )
    late = bit_of(index, 2)
    power = jnp.exp(-rate * (2 * length))
    early_end = jnp.where(late, chip_other_ref[:quarter], chip_ref[:quarter])
    late_start = jnp.where(late, chip_ref[quarter:], chip_other_ref[quarter:])
    early, later = pass_down(early_end, late_start, before, after, power)
    keep_ref[:quarter] = jnp.where(late, later[0], early[0])
    keep_ref[quarter : 2 * quarter] = jnp.where(late, later[1], early[1])
    keep_ref[2 * quarter :] = sums
    send_ref[:quarter] = jnp.where(late, early[0], later[0])
    send_ref[quarter : 2 * quarter] = jnp.where(late, early[1], later[1])
    send_ref[2 * quarter :] = sums


def turn(length, masks, own, other, levels, chip, chip_other, rate):
    shape = ((chip.shape[0] + MODES, LANES), F32)
    return call(
        functools.partial(turn_kernel, length, masks),
        "turn",
        [shape, shape],
        own,
        other,
        *levels,
        chip,
        chip_other,
        rate,
    )


def chip_kernel(length, own_ref, other_ref, core_ref, core_other_ref, rate_ref, keep_ref, send_ref):
    index = lax.axis_index("seq")
    quarter = (own_ref.shape[0] - MODES) // 2
    half = 2 * quarter
    rate = rate_ref[...]
    power = jnp.exp(-rate * length)
    second = bit_of(index, 2)
    own, other = own_ref[:half], other_ref[:half]
    left = jnp.where(second, other, own)
    right = jnp.where(second, own, other)
    before = jnp.concatenate([left[:quarter], right[:quarter]], axis=0)
    after = jnp.concatenate([left[quarter:], right[quarter:]], axis=0)
    late = bit_of(index, 1)
    early_end = jnp.where(late, core_other_ref[:half], core_ref[:half])
    late_start = jnp.where(late, core_ref[half:], core_other_ref[half:])
    early, later = pass_down(early_end, late_start, before, after, power)
    sums = own_ref[half:] + other_ref[half:]
    keep_ref[:half] = jnp.where(late, later[0], early[0])
    keep_ref[half : 2 * half] = jnp.where(late, later[1], early[1])
    keep_ref[2 * half :] = sums
    send_ref[:half] = jnp.where(late, early[0], later[0])
    send_ref[half : 2 * half] = jnp.where(late, early[1], later[1])
    send_ref[2 * half :] = sums


def chip_split(length, own, other, core, core_other, rate):
    shape = ((core.shape[0] + MODES, LANES), F32)
    return call(
        functools.partial(chip_kernel, length),
        "chip_split",
        [shape, shape],
        own,
        other,
        core,
        core_other,
        rate,
    )


def spread(state):
    same = lane_iota((LANES, LANES)) // PER == row_iota((LANES, LANES)) // MODES
    return jnp.where(same, jnp.concatenate([state] * PACK, axis=0), jnp.zeros((), state.dtype))


def carried(high_ref, low_ref, lanes, state):
    high, low = split(state)
    high, low = spread(high), spread(low)
    table = high_ref[:, lanes]
    return jnp.dot(
        jnp.concatenate([table, table, low_ref[:, lanes]], axis=1),
        jnp.concatenate([high, low, high], axis=0),
        preferred_element_type=F32,
    )


CHUNKS = 2


def outputs_kernel(keep, scale, *refs):
    around_ref, sums_refs, decay_ref = refs[0], refs[0:2], refs[2]
    k_ref, v_ref, q_ref, c_ref = refs[3:7]
    fh_ref, fl_ref, bh_ref, bl_ref = refs[7:11]
    length, width = k_ref.shape
    blocks = width // LANES
    pieces = blocks // GROUP
    fore_refs, back_refs = refs[11 : 11 + pieces], refs[11 + pieces : 11 + 2 * pieces]
    rest = refs[11 + 2 * pieces :]
    if not keep:
        rest = rest[4:]
    targets = rest[:4]
    if not keep:
        grad_ref, rest = rest[4], rest[1:]
    scratch, sems = rest[4:8], rest[8]
    out_ref, query_ref, key_ref, value_ref = scratch
    half = kept_half(lax.axis_index("seq"))
    half = half if keep else 1 - half
    copies = []
    each = blocks // CHUNKS
    for chunk in range(CHUNKS):
        for block in range(chunk * each, (chunk + 1) * each):
            lanes = lanes_of(block)
            local = lanes_of(block % GROUP)
            before = around_ref[rows_of(block)]
            after = around_ref[rows_of(blocks + block)]
            mixed = fore_refs[block // GROUP][:, local] + carried(fh_ref, fl_ref, lanes, before)
            out_ref[:, lanes] = (q_ref[:, lanes].astype(F32) * mixed).astype(BF16)
            query_ref[:, lanes] = (c_ref[:, lanes].astype(F32) * mixed).astype(BF16)
            grad = back_refs[block // GROUP][:, local] + carried(bh_ref, bl_ref, lanes, after)
            key_ref[:, lanes] = (grad * v_ref[:, lanes].astype(F32)).astype(BF16)
            value_ref[:, lanes] = (grad * k_ref[:, lanes].astype(F32)).astype(BF16)
        size = each * LANES
        here = pl.ds(chunk * size, size)
        there = pl.ds(pl.multiple_of(half * width + chunk * size, size), size)
        for n in range(4):
            copy = pltpu.make_async_copy(
                scratch[n].at[:, here], targets[n].at[:, there], sems.at[n, chunk]
            )
            copy.start()
            copies.append(copy)
    if not keep:
        base = 2 * blocks * MODES
        sums = sums_refs[0][base:] + sums_refs[1][base:]
        grad_ref[...] = sums * jnp.sqrt(2.0 * decay_ref[...] / MODES) * scale
    for copy in copies:
        copy.wait()


def outputs(keep, scale, around, other, decay, streams, table, fore, back, targets=()):
    length, width = streams[0].shape
    operands = [around, other, decay, *streams, *table, *fore, *back]
    shapes = [jax.ShapeDtypeStruct((length, 2 * width), BF16)] * 4
    spaces = [pltpu.HBM] * 4
    if not keep:
        shapes.append(jax.ShapeDtypeStruct(decay.shape, F32))
        spaces.append(pltpu.VMEM)
    ins = [pltpu.VMEM] * len(operands) + [pltpu.HBM] * len(targets)
    return pl.pallas_call(
        functools.partial(outputs_kernel, keep, scale),
        in_specs=[pl.BlockSpec(memory_space=space) for space in ins],
        out_specs=[pl.BlockSpec(memory_space=space) for space in spaces],
        out_shape=shapes,
        scratch_shapes=[pltpu.VMEM((length, width), BF16)] * 4
        + [pltpu.SemaphoreType.DMA((4, CHUNKS))],
        input_output_aliases={len(operands) + n: n for n in range(len(targets))},
        compiler_params=pltpu.CompilerParams(vmem_limit_bytes=16 << 20),
        name="outputs_keep" if keep else "outputs_sent",
    )(*operands, *targets)


def tie(*values):
    return lax.optimization_barrier(values)


def per_device(query, key, value, cotangent, decay, residue):
    length, total = query.shape
    blocks = total // LANES // 2
    count = lax.axis_size("seq")
    masks = [1 << i for i in range(2, count.bit_length() - 1)]
    decay, residue = decay.T, residue.T

    def swap(array, mask):
        flip = mask | 1
        return lax.ppermute(array, "seq", [(i, i ^ flip) for i in range(count)])

    first, decay, sent, kept = send_states(key, value, query, cotangent, decay)
    core_send, rate_sent, gated_sent, upstream_sent = first
    core_send, decay, gated_sent, upstream_sent, *kept = tie(
        core_send, decay, gated_sent, upstream_sent, *kept
    )
    core_other = swap(core_send, 1)
    core, rate, gated, upstream = keep_states(decay, kept)
    lags = [lag_part(False, gated_sent, upstream_sent, rate_sent, 0, GROUP)]
    core_other, lags[0] = tie(core_other, lags[0])
    chip_send, chip, core_sums = core_join(length, core, core_other, rate)
    chip_send, gated, upstream, gated_sent = tie(chip_send, gated, upstream, gated_sent)
    chip_other = swap(chip_send, 2)
    lags.append(lag_part(False, gated_sent, upstream_sent, rate_sent, GROUP, blocks - GROUP))
    lags.append(lag_part(True, gated, upstream, rate, 0, blocks))
    message = plane_join(length, chip, chip_other, [core_sums, *lags], rate)

    message, rate, rate_sent = tie(message, rate, rate_sent)
    weight, *table = tables(True, decay, residue, rate, length)
    weight_sent, *table_sent = tables(False, decay, residue, rate_sent, length)
    tasks = [
        (values, rates, weights, reverse, start)
        for rates, weights, pair in [
            (rate, weight, (gated, upstream)),
            (rate_sent, weight_sent, (gated_sent, upstream_sent)),
        ]
        for reverse, values in zip((False, True), pair)
        for start in range(0, blocks, GROUP)
    ]
    scans = []

    def some(number, *held):
        todo = tasks[len(scans) : len(scans) + number]
        values, *held = tie([task[0] for task in todo], *held)
        scans.extend(scan_part([(x, *task[1:]) for x, task in zip(values, todo)]))
        return held

    levels = []
    for mask in masks[:-1]:
        other = swap(message, mask)
        if mask == masks[0]:
            (message,) = some(2, message)
            other, *scans[-2:] = tie(other, *scans[-2:])
        levels.append(other)
        message = line_join(length, mask, mask == masks[-2], message, other, rate)
    top = swap(message, masks[-1])
    (message,) = some(3, message)
    top, *scans[-3:] = tie(top, *scans[-3:])
    keep, send = turn(length, masks, message, top, levels, chip, chip_other, rate)
    arrived = swap(send, 2)
    (send,) = some(3, send)
    arrived, *scans[-3:] = tie(arrived, *scans[-3:])
    own, send = chip_split(length, keep, arrived, core, core_other, rate)
    other = swap(send, 1)
    scale = 1.0 / math.sqrt(length * count)
    pieces = blocks // GROUP
    fore, back, fore_sent, back_sent = (scans[i * pieces : (i + 1) * pieces] for i in range(4))
    wide = outputs(True, scale, own, own, decay, kept, table, fore, back)
    *wide, grad = outputs(
        False, scale, other, own, decay, sent, table_sent, fore_sent, back_sent, wide
    )
    return (*wide, grad.T)


def solution(mesh):
    rows = P(("grp", "seq"), None)
    return jax.shard_map(
        per_device,
        mesh=mesh,
        in_specs=(rows, rows, rows, rows, P(), P()),
        out_specs=(rows, rows, rows, rows, P("grp", None)),
        check_vma=False,
    )
```

```python
import functools
import math

import jax
import jax.numpy as jnp
from jax import lax
from jax.experimental import pallas as pl
from jax.experimental.pallas import tpu as pltpu
from jax.sharding import PartitionSpec as P

PER = 16
MODES = 16
LANES = 128
PACK = LANES // PER
F32 = jnp.float32
BF16 = jnp.bfloat16


def lane_iota(shape):
    return lax.broadcasted_iota(jnp.int32, shape, 1)


def row_iota(shape):
    return lax.broadcasted_iota(jnp.int32, shape, 0)


def split(value):
    high = value.astype(BF16)
    return high, (value - high.astype(F32)).astype(BF16)


def lanes_of(block):
    if isinstance(block, int):
        return slice(block * LANES, (block + 1) * LANES)
    return pl.ds(pl.multiple_of(block * LANES, LANES), LANES)


def rows_of(block):
    if isinstance(block, int):
        return slice(block * MODES, (block + 1) * MODES)
    return pl.ds(pl.multiple_of(block * MODES, MODES), MODES)


def over_blocks(count, step, body):
    if step == count:
        for block in range(count):
            body(block, block, 0)
        return

    def some(i, carry):
        for n in range(step):
            body(i * step + n, n, i * step)
        return carry

    lax.fori_loop(0, count // step, some, 0)


def turned(by_filter, block):
    if isinstance(block, int):
        return by_filter
    return pltpu.roll(by_filter, (LANES - block * PACK) % LANES, 1)


STEP = 8


def dot_split(left, right):
    return jnp.dot(
        jnp.concatenate([left[0], left[0], left[1]], axis=1),
        jnp.concatenate([right[0], right[1], right[0]], axis=0),
        preferred_element_type=F32,
    )


def own_group(stack):
    group = lane_iota((MODES, LANES)) // PER
    total = stack[rows_of(0)]
    for g in range(1, PACK):
        total = jnp.where(group == g, stack[rows_of(g)], total)
    return total


def columns(by_filter, first):
    return jnp.concatenate(
        [
            jnp.broadcast_to(by_filter[:, g : g + 1], (MODES, LANES))
            for g in range(first, first + PACK)
        ],
        axis=0,
    )


def filter_sums(stack, first):
    high, low = split(stack)
    spot = lane_iota((LANES, LANES)) % PACK == row_iota((LANES, LANES)) // PER
    spot = spot.astype(F32).astype(BF16)
    sums = jnp.dot(
        jnp.concatenate([high, low], axis=1),
        jnp.concatenate([spot, spot], axis=0),
        preferred_element_type=F32,
    )
    block = lane_iota((MODES, LANES)) // PACK - first
    total = jnp.zeros((MODES, LANES), F32)
    for i in range(stack.shape[0] // MODES):
        total = total + jnp.where(block == i, sums[rows_of(i)], 0.0)
    return total


def bit_of(index, mask):
    return (index & mask) != 0


def kept_half(index):
    for shift in (8, 4, 2, 1):
        index = index ^ (index >> shift)
    return index & 1


def call(kernel, name, outs, *operands, scratch=(), outs_in=None, ins_in=None):
    ins_in = ins_in or [pltpu.VMEM] * len(operands)
    outs_in = outs_in or [pltpu.VMEM] * len(outs)
    return pl.pallas_call(
        kernel,
        in_specs=[pl.BlockSpec(memory_space=space) for space in ins_in],
        out_specs=[pl.BlockSpec(memory_space=space) for space in outs_in],
        out_shape=[jax.ShapeDtypeStruct(shape, dtype) for shape, dtype in outs],
        scratch_shapes=list(scratch),
        compiler_params=pltpu.CompilerParams(vmem_limit_bytes=16 << 20),
        name=name,
    )(*operands)


def of_half(by_filter, half):
    return jnp.where(half == 0, by_filter, pltpu.roll(by_filter, LANES // 2, 1))


def power_tables(decay, block, length):
    time = lane_iota((LANES, length)).astype(F32)
    rate = columns(decay, block * PACK)
    return rate, jnp.exp(-rate * (length - 1.0 - time)), jnp.exp(-rate * time)


def block_states(block, ends, starts, streams, state_ref, gated_ref, upstream_ref):
    k_ref, v_ref, q_ref, c_ref = streams
    blocks = gated_ref.shape[1] // LANES
    lanes = lanes_of(block)
    gated = k_ref[:, lanes].astype(F32) * v_ref[:, lanes].astype(F32)
    upstream = q_ref[:, lanes].astype(F32) * c_ref[:, lanes].astype(F32)
    gated_ref[:, lanes] = gated
    upstream_ref[:, lanes] = upstream
    state_ref[rows_of(block)] = own_group(dot_split(ends, split(gated)))
    state_ref[rows_of(block + blocks)] = own_group(dot_split(starts, split(upstream)))


def send_states_kernel(*refs):
    sources, decay_hbm = refs[:4], refs[4]
    state_ref, rate_ref, gated_ref, upstream_ref, decay_ref = refs[5:10]
    sent, kept = refs[10:14], refs[14:18]
    table_ref, sems, decay_sem = refs[18:]
    half = kept_half(lax.axis_index("seq"))
    length, width = gated_ref.shape
    blocks = width // LANES
    decay_copy = pltpu.make_async_copy(decay_hbm, decay_ref, decay_sem)
    decay_copy.start()
    copies = []
    for role, targets in enumerate([sent, kept]):
        at = pl.multiple_of((half if role else 1 - half) * width, width)
        for n in range(4):
            copy = pltpu.make_async_copy(
                sources[n].at[:, pl.ds(at, width)], targets[n], sems.at[role, n]
            )
            copies.append(copy)
    for copy in copies[:4]:
        copy.start()
    decay_copy.wait()
    for copy in copies[4:]:
        copy.start()
    decay = of_half(decay_ref[...], 1 - half)
    def make(block, place, first):
        rate, *powers = power_tables(turned(decay, first), place, length)
        rate_ref[rows_of(block)] = own_group(rate)
        for n, power in enumerate(powers):
            table_ref[2 * n, :, lanes_of(block)], table_ref[2 * n + 1, :, lanes_of(block)] = split(
                power
            )

    over_blocks(blocks, STEP, make)
    for copy in copies[:4]:
        copy.wait()

    def use(block, place, first):
        high, low, start_high, start_low = (table_ref[n, :, lanes_of(block)] for n in range(4))
        block_states(
            block,
            (high, low),
            (start_high, start_low),
            sent,
            state_ref,
            gated_ref,
            upstream_ref,
        )

    over_blocks(blocks, STEP, use)
    for copy in copies[4:]:
        copy.wait()


def keep_states_kernel(decay_ref, *refs):
    streams = refs[:4]
    state_ref, rate_ref, gated_ref, upstream_ref = refs[4:]
    decay = of_half(decay_ref[...], kept_half(lax.axis_index("seq")))
    length, width = gated_ref.shape

    def both(block, place, first):
        rate, ends, starts = power_tables(turned(decay, first), place, length)
        rate_ref[rows_of(block)] = own_group(rate)
        block_states(
            block, split(ends), split(starts), streams, state_ref, gated_ref, upstream_ref
        )

    over_blocks(width // LANES, STEP, both)


def state_shapes(length, width):
    blocks = width // LANES
    return [
        ((2 * blocks * MODES, LANES), F32),
        ((blocks * MODES, LANES), F32),
        ((length, width), F32),
        ((length, width), F32),
    ]


def send_states(k, v, q, c, decay):
    length, total = k.shape
    arrays = [pltpu.with_memory_space_constraint(x, pltpu.HBM) for x in (k, v, q, c, decay)]
    outs = call(
        send_states_kernel,
        "send_states",
        state_shapes(length, total // 2)
        + [(decay.shape, F32)]
        + [((length, total // 2), k.dtype)] * 8,
        *arrays,
        scratch=[
            pltpu.VMEM((4, LANES, length * total // 2 // LANES), BF16),
            pltpu.SemaphoreType.DMA((2, 4)),
            pltpu.SemaphoreType.DMA,
        ],
        ins_in=[pltpu.HBM] * 5,
    )
    return outs[:4], outs[4], outs[5:9], outs[9:]


def keep_states(decay, streams):
    return call(
        keep_states_kernel, "keep_states", state_shapes(*streams[0].shape), decay, *streams
    )


def tables_kernel(keep, decay_ref, residue_ref, rate_ref, *refs):
    weight_ref, fh_ref, fl_ref, bh_ref, bl_ref = refs
    length, width = fh_ref.shape
    half = kept_half(lax.axis_index("seq"))
    weights = residue_ref[...] * jnp.sqrt(2.0 * decay_ref[...] / MODES)
    weights = of_half(weights, half if keep else 1 - half)
    pick = lane_iota((MODES, LANES)) % MODES == row_iota((MODES, LANES))
    time = row_iota((MODES, LANES)).astype(F32)

    def across(stack):
        return jnp.sum(jnp.where(pick, stack, 0.0), axis=0, keepdims=True)

    for block in range(width // LANES):
        lanes = lanes_of(block)
        weight = own_group(columns(weights, block * PACK))
        weight_ref[rows_of(block)] = weight
        rate = jnp.broadcast_to(across(rate_ref[rows_of(block)]), (MODES, LANES))
        weight = jnp.broadcast_to(across(weight), (MODES, LANES))
        step = jnp.exp(-rate * MODES)
        fore = weight * jnp.exp(-rate * (time + 1.0))
        back = weight * jnp.exp(-rate * (MODES - time))
        for i in range(length // MODES):
            rows = rows_of(i)
            fh_ref[rows, lanes], fl_ref[rows, lanes] = split(fore)
            rows = rows_of(length // MODES - 1 - i)
            bh_ref[rows, lanes], bl_ref[rows, lanes] = split(back)
            fore = fore * step
            back = back * step


def tables(keep, decay, residue, rate, length):
    width = rate.shape[0] // MODES * LANES
    return call(
        functools.partial(tables_kernel, keep),
        "tables",
        [(rate.shape, F32)] + [((length, width), BF16)] * 4,
        decay,
        residue,
        rate,
    )


GROUP = 2


def lag_kernel(keep, first, count, gated_ref, upstream_ref, rate_ref, *refs):
    out_ref = refs[-1]
    length, width = gated_ref.shape
    half = kept_half(lax.axis_index("seq"))
    offset = (half if keep else 1 - half) * (width // LANES)
    out = jnp.zeros((MODES, LANES), F32)
    for cross_ref in refs[:-1]:
        out = filter_sums(cross_ref[...], offset)
    for start in range(first, first + count, GROUP):
        blocks = range(start, start + GROUP)
        decays = [jnp.exp(-rate_ref[rows_of(block)]) for block in blocks]

        def eight(i, carry, blocks=blocks, decays=decays):
            states, totals = list(carry[0]), list(carry[1])
            base = pl.multiple_of(i * 8, 8)
            xs = [gated_ref[pl.ds(base, 8), lanes_of(block)] for block in blocks]
            us = [upstream_ref[pl.ds(base, 8), lanes_of(block)] for block in blocks]
            for j in range(8):
                for n in range(GROUP):
                    x = jnp.broadcast_to(xs[n][j : j + 1], (MODES, LANES))
                    u = jnp.broadcast_to(us[n][j : j + 1], (MODES, LANES))
                    states[n] = states[n] * decays[n] + x
                    totals[n] = totals[n] + states[n] * u
            return tuple(states), tuple(totals)

        zeros = (jnp.zeros((MODES, LANES), F32),) * GROUP
        _, totals = lax.fori_loop(0, length // 8, eight, (zeros, zeros), unroll=True)
        out = out + filter_sums(jnp.concatenate(totals, axis=0), offset + start)
    out_ref[...] = out


def lag_part(keep, gated, upstream, rate, first, count, *cross):
    return call(
        functools.partial(lag_kernel, keep, first, count),
        "lag_part",
        [((MODES, LANES), F32)],
        gated,
        upstream,
        rate,
        *cross,
    )[0]


def fold(first, second, shift, row):
    low = (row & shift) == 0
    kept = jnp.where(low, first, second)
    moved = jnp.where(low, second, first)
    return kept + pltpu.roll(moved, shift, 0)


def scan_kernel(tasks, *refs):
    row = row_iota((8, LANES))
    for n, (reverse, start) in enumerate(tasks):
        in_ref, rate_ref, weight_ref = refs[3 * n : 3 * n + 3]
        out_ref = refs[3 * len(tasks) + n]
        length = in_ref.shape[0]
        blocks = range(start, start + GROUP)
        decays = [jnp.exp(-rate_ref[rows_of(block)]) for block in blocks]
        weights = [weight_ref[rows_of(block)] for block in blocks]

        def eight(
            i,
            carry,
            reverse=reverse,
            blocks=blocks,
            decays=decays,
            weights=weights,
            in_ref=in_ref,
            out_ref=out_ref,
        ):
            states = list(carry)
            at = length // 8 - 1 - i if reverse else i
            base = pl.multiple_of(at * 8, 8)
            rows = [in_ref[pl.ds(base, 8), lanes_of(block)] for block in blocks]
            parts = [[None] * 8 for _ in blocks]
            for j in reversed(range(8)) if reverse else range(8):
                for n in range(GROUP):
                    x = jnp.broadcast_to(rows[n][j : j + 1], (MODES, LANES))
                    states[n] = states[n] * decays[n] + x
                    product = states[n] * weights[n]
                    parts[n][j] = product[:8] + product[8:]
            for n, block in enumerate(blocks):
                part = parts[n]
                four = [fold(part[2 * j], part[2 * j + 1], 1, row) for j in range(4)]
                two = [fold(four[2 * j], four[2 * j + 1], 2, row) for j in range(2)]
                place = lanes_of(n)
                out_ref[pl.ds(base, 8), place] = fold(two[0], two[1], 4, row)
            return tuple(states)

        zeros = (jnp.zeros((MODES, LANES), F32),) * GROUP
        lax.fori_loop(0, length // 8, eight, zeros, unroll=True)


def scan_part(tasks):
    operands = [x for task in tasks for x in task[:3]]
    return call(
        functools.partial(scan_kernel, [task[3:] for task in tasks]),
        "scan",
        [((tasks[0][0].shape[0], GROUP * LANES), F32)] * len(tasks),
        *operands,
    )


def join(own, other, late, power, step_decay):
    half = power.shape[0]
    own_end, own_start = own[:half], own[half : 2 * half]
    other_end, other_start = other[:half], other[half : 2 * half]
    early_end = jnp.where(late, other_end, own_end)
    late_end = jnp.where(late, own_end, other_end)
    early_start = jnp.where(late, other_start, own_start)
    late_start = jnp.where(late, own_start, other_start)
    end = late_end + power * early_end
    start = early_start + power * late_start
    return end, start, early_end * late_start * step_decay


def pass_down(first, second, before, after, power):
    early = (before, second + power * after)
    late = (first + power * before, after)
    return early, late


def quarter_of(index, ref):
    rows = ref.shape[0] // 2
    return pl.ds(pl.multiple_of(((index >> 1) & 1) * rows, rows), rows)


def first_block(index, rows):
    return (kept_half(index) * 2 + ((index >> 1) & 1)) * (rows // MODES)


def core_kernel(length, own_ref, other_ref, rate_ref, send_ref, keep_ref, cross_ref):
    index = lax.axis_index("seq")
    half = own_ref.shape[0] // 2
    quarter = half // 2
    rate = rate_ref[...]
    end, start, cross = join(
        own_ref[...],
        other_ref[...],
        bit_of(index, 1),
        jnp.exp(-rate * length),
        jnp.exp(-rate),
    )
    second = bit_of(index, 2)
    keep_ref[:quarter] = jnp.where(second, end[quarter:], end[:quarter])
    keep_ref[quarter:] = jnp.where(second, start[quarter:], start[:quarter])
    send_ref[:quarter] = jnp.where(second, end[:quarter], end[quarter:])
    send_ref[quarter:] = jnp.where(second, start[:quarter], start[quarter:])
    cross_ref[...] = cross


def core_join(length, own, other, rate):
    half = ((own.shape[0] // 2, LANES), F32)
    return call(
        functools.partial(core_kernel, length),
        "core_join",
        [half, half, half],
        own,
        other,
        rate,
    )


def plane_kernel(length, own_ref, other_ref, *refs):
    *sums_refs, rate_ref, out_ref = refs
    index = lax.axis_index("seq")
    quarter = own_ref.shape[0] // 2
    rate = rate_ref[quarter_of(index, rate_ref)]
    end, start, cross = join(
        own_ref[...],
        other_ref[...],
        bit_of(index, 2),
        jnp.exp(-rate * (2 * length)),
        jnp.exp(-rate),
    )
    out_ref[:quarter] = end
    out_ref[quarter : 2 * quarter] = start
    sums = filter_sums(cross, first_block(index, quarter))
    for ref in sums_refs:
        sums = sums + ref[...]
    out_ref[2 * quarter :] = sums


def plane_join(length, own, other, sums, rate):
    return call(
        functools.partial(plane_kernel, length),
        "plane_join",
        [((own.shape[0] + MODES, LANES), F32)],
        own,
        other,
        *sums,
        rate,
    )[0]


def line_kernel(length, mask, final, own_ref, other_ref, rate_ref, out_ref):
    index = lax.axis_index("seq")
    quarter = (own_ref.shape[0] - MODES) // 2
    rate = rate_ref[quarter_of(index, rate_ref)]
    end, start, cross = join(
        own_ref[...],
        other_ref[...],
        bit_of(index, mask),
        jnp.exp(-rate * (mask * length)),
        jnp.exp(-rate),
    )
    sums = own_ref[2 * quarter :] + other_ref[2 * quarter :] + filter_sums(cross, first_block(index, quarter))
    if final:
        out_ref[:quarter] = jnp.where(bit_of(index, 2 * mask), start, end)
        out_ref[quarter:] = sums
    else:
        out_ref[:quarter] = end
        out_ref[quarter : 2 * quarter] = start
        out_ref[2 * quarter :] = sums


def line_join(length, mask, final, own, other, rate):
    quarter = (own.shape[0] - MODES) // 2
    count = (quarter if final else 2 * quarter) + MODES
    return call(
        functools.partial(line_kernel, length, mask, final),
        "line_join",
        [((count, LANES), F32)],
        own,
        other,
        rate,
    )[0]


def turn_kernel(length, masks, own_ref, other_ref, *refs):
    levels = refs[: len(masks) - 1]
    chip_ref, chip_other_ref, rate_ref, keep_ref, send_ref = refs[len(masks) - 1 :]
    index = lax.axis_index("seq")
    quarter = own_ref.shape[0] - MODES
    rate = rate_ref[quarter_of(index, rate_ref)]
    own, other = own_ref[:quarter], other_ref[:quarter]
    late = bit_of(index, masks[-1])
    cross = own * other * jnp.exp(-rate)
    sums = own_ref[quarter:] + other_ref[quarter:] + filter_sums(cross, first_block(index, quarter))
    before = jnp.where(late, other, 0.0)
    after = jnp.where(late, 0.0, other)
    for mask, level in reversed(list(zip(masks[:-1], levels))):
        late = bit_of(index, mask)
        power = jnp.exp(-rate * (mask * length))
        before, after = (
            jnp.where(late, level[:quarter] + power * before, before),
            jnp.where(late, after, level[quarter : 2 * quarter] + power * after),
        )
    late = bit_of(index, 2)
    power = jnp.exp(-rate * (2 * length))
    early_end = jnp.where(late, chip_other_ref[:quarter], chip_ref[:quarter])
    late_start = jnp.where(late, chip_ref[quarter:], chip_other_ref[quarter:])
    early, later = pass_down(early_end, late_start, before, after, power)
    keep_ref[:quarter] = jnp.where(late, later[0], early[0])
    keep_ref[quarter : 2 * quarter] = jnp.where(late, later[1], early[1])
    keep_ref[2 * quarter :] = sums
    send_ref[:quarter] = jnp.where(late, early[0], later[0])
    send_ref[quarter : 2 * quarter] = jnp.where(late, early[1], later[1])
    send_ref[2 * quarter :] = sums


def turn(length, masks, own, other, levels, chip, chip_other, rate):
    shape = ((chip.shape[0] + MODES, LANES), F32)
    return call(
        functools.partial(turn_kernel, length, masks),
        "turn",
        [shape, shape],
        own,
        other,
        *levels,
        chip,
        chip_other,
        rate,
    )


def chip_kernel(length, own_ref, other_ref, core_ref, core_other_ref, rate_ref, keep_ref, send_ref):
    index = lax.axis_index("seq")
    quarter = (own_ref.shape[0] - MODES) // 2
    half = 2 * quarter
    rate = rate_ref[...]
    power = jnp.exp(-rate * length)
    second = bit_of(index, 2)
    own, other = own_ref[:half], other_ref[:half]
    left = jnp.where(second, other, own)
    right = jnp.where(second, own, other)
    before = jnp.concatenate([left[:quarter], right[:quarter]], axis=0)
    after = jnp.concatenate([left[quarter:], right[quarter:]], axis=0)
    late = bit_of(index, 1)
    early_end = jnp.where(late, core_other_ref[:half], core_ref[:half])
    late_start = jnp.where(late, core_ref[half:], core_other_ref[half:])
    early, later = pass_down(early_end, late_start, before, after, power)
    sums = own_ref[half:] + other_ref[half:]
    keep_ref[:half] = jnp.where(late, later[0], early[0])
    keep_ref[half : 2 * half] = jnp.where(late, later[1], early[1])
    keep_ref[2 * half :] = sums
    send_ref[:half] = jnp.where(late, early[0], later[0])
    send_ref[half : 2 * half] = jnp.where(late, early[1], later[1])
    send_ref[2 * half :] = sums


def chip_split(length, own, other, core, core_other, rate):
    shape = ((core.shape[0] + MODES, LANES), F32)
    return call(
        functools.partial(chip_kernel, length),
        "chip_split",
        [shape, shape],
        own,
        other,
        core,
        core_other,
        rate,
    )


def spread(state):
    same = lane_iota((LANES, LANES)) // PER == row_iota((LANES, LANES)) // MODES
    return jnp.where(same, jnp.concatenate([state] * PACK, axis=0), jnp.zeros((), state.dtype))


def carried(high_ref, low_ref, lanes, state):
    high, low = split(state)
    high, low = spread(high), spread(low)
    return dot_split((high_ref[:, lanes], low_ref[:, lanes]), (high, low))


CHUNKS = 4


def write_block(block, blocks, refs, results):
    around_ref, k_ref, v_ref, q_ref, c_ref, fh_ref, fl_ref, bh_ref, bl_ref = refs[:9]
    pieces = blocks // GROUP
    fore_refs, back_refs = refs[9 : 9 + pieces], refs[9 + pieces : 9 + 2 * pieces]
    out_ref, query_ref, key_ref, value_ref = results
    lanes = lanes_of(block)
    local = lanes_of(block % GROUP)
    before = around_ref[rows_of(block)]
    after = around_ref[rows_of(blocks + block)]
    mixed = fore_refs[block // GROUP][:, local] + carried(fh_ref, fl_ref, lanes, before)
    out_ref[:, lanes] = (q_ref[:, lanes].astype(F32) * mixed).astype(BF16)
    query_ref[:, lanes] = (c_ref[:, lanes].astype(F32) * mixed).astype(BF16)
    grad = back_refs[block // GROUP][:, local] + carried(bh_ref, bl_ref, lanes, after)
    key_ref[:, lanes] = (grad * v_ref[:, lanes].astype(F32)).astype(BF16)
    value_ref[:, lanes] = (grad * k_ref[:, lanes].astype(F32)).astype(BF16)


def keep_outputs_kernel(*refs):
    blocks = refs[1].shape[1] // LANES
    for block in range(blocks):
        write_block(block, blocks, refs[:-4], refs[-4:])


def keep_outputs(operands):
    shape = (operands[1].shape, BF16)
    return call(keep_outputs_kernel, "keep_outputs", [shape] * 4, *operands)


def sent_outputs_kernel(scale, *refs):
    kept, own_ref, decay_ref = refs[:4], refs[4], refs[5]
    targets, grad_ref = refs[-11:-7], refs[-7]
    scratch, kept_sems, sems = refs[-6:-2], refs[-2], refs[-1]
    refs = refs[6:-11]
    around_ref = refs[0]
    width = refs[1].shape[1]
    blocks = width // LANES
    half = kept_half(lax.axis_index("seq"))
    copies = []

    def send(sources, which, start, size, sems):
        at = pl.multiple_of(which * width + start, size)
        for n in range(4):
            copy = pltpu.make_async_copy(
                sources[n].at[:, pl.ds(start, size)], targets[n].at[:, pl.ds(at, size)], sems.at[n]
            )
            copy.start()
            copies.append(copy)

    send(kept, half, 0, width, kept_sems)
    each = blocks // CHUNKS
    for chunk in range(CHUNKS):
        for block in range(chunk * each, (chunk + 1) * each):
            write_block(block, blocks, refs, scratch)
        send(scratch, 1 - half, chunk * each * LANES, each * LANES, sems.at[chunk])
    base = 2 * blocks * MODES
    sums = own_ref[base:] + around_ref[base:]
    grad_ref[...] = sums * jnp.sqrt(2.0 * decay_ref[...] / MODES) * scale
    for copy in copies:
        copy.wait()


def sent_outputs(scale, kept, own, decay, operands):
    length, width = kept[0].shape
    return call(
        functools.partial(sent_outputs_kernel, scale),
        "sent_outputs",
        [((length, 2 * width), BF16)] * 4 + [(decay.shape, F32)],
        *kept,
        own,
        decay,
        *operands,
        scratch=[pltpu.VMEM((length, width), BF16)] * 4
        + [pltpu.SemaphoreType.DMA((4,)), pltpu.SemaphoreType.DMA((CHUNKS, 4))],
        outs_in=[pltpu.HBM] * 4 + [pltpu.VMEM],
    )


FILL = (4, 6, 6)


def tie(*values):
    return lax.optimization_barrier(values)


def per_device(query, key, value, cotangent, decay, residue):
    length, total = query.shape
    blocks = total // LANES // 2
    count = lax.axis_size("seq")
    masks = [1 << i for i in range(2, count.bit_length() - 1)]
    decay, residue = decay.T, residue.T

    def swap(array, mask):
        flip = mask | 1
        return lax.ppermute(array, "seq", [(i, i ^ flip) for i in range(count)])

    first, decay, sent, kept = send_states(key, value, query, cotangent, decay)
    core_send, rate_sent, gated_sent, upstream_sent = first
    core_send, decay, gated_sent, upstream_sent, *kept = tie(
        core_send, decay, gated_sent, upstream_sent, *kept
    )
    core_other = swap(core_send, 1)
    core, rate, gated, upstream = keep_states(decay, kept)
    core_other, core = tie(core_other, core)
    chip_send, chip, core_cross = core_join(length, core, core_other, rate)
    chip_send, gated, upstream, gated_sent = tie(chip_send, gated, upstream, gated_sent)
    chip_other = swap(chip_send, 2)
    lags = [
        lag_part(False, gated_sent, upstream_sent, rate_sent, 0, blocks),
        lag_part(True, gated, upstream, rate, 0, blocks, core_cross),
    ]
    message = plane_join(length, chip, chip_other, lags, rate)

    message, rate, rate_sent = tie(message, rate, rate_sent)
    weight, *table = tables(True, decay, residue, rate, length)
    weight_sent, *table_sent = tables(False, decay, residue, rate_sent, length)
    tasks = [
        (values, rates, weights, reverse, start)
        for rates, weights, pair in [
            (rate, weight, (gated, upstream)),
            (rate_sent, weight_sent, (gated_sent, upstream_sent)),
        ]
        for reverse, values in zip((False, True), pair)
        for start in range(0, blocks, GROUP)
    ]
    scans = []

    def fill(number, held, *more):
        todo = tasks[len(scans) : len(scans) + number]
        held, *values = tie(held, *[task[0] for task in todo])
        scans.extend(scan_part([(x, *task[1:]) for x, task in zip(values, todo)]))

        def after(arrived):
            arrived, *scans[-number:] = tie(arrived, *scans[-number:])
            if more:
                arrived, *_ = tie(arrived, *more)
            return arrived

        return held, after

    levels = []
    for mask in masks[:-1]:
        if mask == masks[0]:
            message, after = fill(FILL[0], message, table[0], table_sent[0])
            levels.append(after(swap(message, mask)))
        else:
            levels.append(swap(message, mask))
        message = line_join(length, mask, mask == masks[-2], message, levels[-1], rate)
    message, after = fill(FILL[1], message)
    top = after(swap(message, masks[-1]))
    keep, send = turn(length, masks, message, top, levels, chip, chip_other, rate)
    send, after = fill(FILL[2], send)
    arrived = after(swap(send, 2))
    own, send = chip_split(length, keep, arrived, core, core_other, rate)
    rest = len(tasks) - len(scans)
    if rest:
        send, after = fill(rest, send)
        other = after(swap(send, 1))
    else:
        other = swap(send, 1)
    scale = 1.0 / math.sqrt(length * count)
    cut = len(scans) // 2
    done = keep_outputs([own, *kept, *table, *scans[:cut]])
    *wide, grad = sent_outputs(scale, done, own, decay, [other, *sent, *table_sent, *scans[cut:]])
    return (*wide, grad.T)


def solution(mesh):
    rows = P(("grp", "seq"), None)
    return jax.shard_map(
        per_device,
        mesh=mesh,
        in_specs=(rows, rows, rows, rows, P(), P()),
        out_specs=(rows, rows, rows, rows, P("grp", None)),
        check_vma=False,
    )
```

```python
import functools
import math

import jax
import jax.numpy as jnp
from jax import lax
from jax.experimental import pallas as pl
from jax.experimental.pallas import tpu as pltpu
from jax.sharding import PartitionSpec as P

PER = 16
MODES = 16
LANES = 128
PACK = LANES // PER
F32 = jnp.float32
BF16 = jnp.bfloat16


def lane_iota(shape):
    return lax.broadcasted_iota(jnp.int32, shape, 1)


def row_iota(shape):
    return lax.broadcasted_iota(jnp.int32, shape, 0)


def split(value):
    high = value.astype(BF16)
    return high, (value - high.astype(F32)).astype(BF16)


def lanes_of(block):
    if isinstance(block, int):
        return slice(block * LANES, (block + 1) * LANES)
    return pl.ds(pl.multiple_of(block * LANES, LANES), LANES)


def rows_of(block):
    if isinstance(block, int):
        return slice(block * MODES, (block + 1) * MODES)
    return pl.ds(pl.multiple_of(block * MODES, MODES), MODES)


def over_blocks(count, step, body):
    if step == count:
        for block in range(count):
            body(block, block, 0)
        return

    def some(i, carry):
        for n in range(step):
            body(i * step + n, n, i * step)
        return carry

    lax.fori_loop(0, count // step, some, 0)


def turned(by_filter, block):
    if isinstance(block, int):
        return by_filter
    return pltpu.roll(by_filter, (LANES - block * PACK) % LANES, 1)


STEP = 8


def dot_split(left, right):
    return jnp.dot(
        jnp.concatenate([left[0], left[0], left[1]], axis=1),
        jnp.concatenate([right[0], right[1], right[0]], axis=0),
        preferred_element_type=F32,
    )


def own_group(stack):
    group = lane_iota((MODES, LANES)) // PER
    total = stack[rows_of(0)]
    for g in range(1, PACK):
        total = jnp.where(group == g, stack[rows_of(g)], total)
    return total


def columns(by_filter, first):
    return jnp.concatenate(
        [
            jnp.broadcast_to(by_filter[:, g : g + 1], (MODES, LANES))
            for g in range(first, first + PACK)
        ],
        axis=0,
    )


def filter_sums(stack, first):
    high, low = split(stack)
    spot = lane_iota((LANES, LANES)) % PACK == row_iota((LANES, LANES)) // PER
    spot = spot.astype(F32).astype(BF16)
    sums = jnp.dot(
        jnp.concatenate([high, low], axis=1),
        jnp.concatenate([spot, spot], axis=0),
        preferred_element_type=F32,
    )
    block = lane_iota((MODES, LANES)) // PACK - first
    total = jnp.zeros((MODES, LANES), F32)
    for i in range(stack.shape[0] // MODES):
        total = total + jnp.where(block == i, sums[rows_of(i)], 0.0)
    return total


def bit_of(index, mask):
    return (index & mask) != 0


def kept_half(index):
    for shift in (8, 4, 2, 1):
        index = index ^ (index >> shift)
    return index & 1


def call(kernel, name, outs, *operands, scratch=(), outs_in=None, ins_in=None):
    ins_in = ins_in or [pltpu.VMEM] * len(operands)
    outs_in = outs_in or [pltpu.VMEM] * len(outs)
    return pl.pallas_call(
        kernel,
        in_specs=[pl.BlockSpec(memory_space=space) for space in ins_in],
        out_specs=[pl.BlockSpec(memory_space=space) for space in outs_in],
        out_shape=[jax.ShapeDtypeStruct(shape, dtype) for shape, dtype in outs],
        scratch_shapes=list(scratch),
        compiler_params=pltpu.CompilerParams(vmem_limit_bytes=16 << 20),
        name=name,
    )(*operands)


def of_half(by_filter, half):
    return jnp.where(half == 0, by_filter, pltpu.roll(by_filter, LANES // 2, 1))


def power_tables(decay, block, length):
    time = lane_iota((LANES, length)).astype(F32)
    rate = columns(decay, block * PACK)
    return rate, jnp.exp(-rate * (length - 1.0 - time)), jnp.exp(-rate * time)


def block_states(block, ends, starts, streams, state_ref, gated_ref, upstream_ref):
    k_ref, v_ref, q_ref, c_ref = streams
    length, width = k_ref.shape
    blocks = width // LANES
    lanes = lanes_of(block)
    gated = k_ref[:, lanes].astype(F32) * v_ref[:, lanes].astype(F32)
    upstream = q_ref[:, lanes].astype(F32) * c_ref[:, lanes].astype(F32)
    gated_ref[pl.ds(block, length, stride=blocks), :] = gated
    upstream_ref[pl.ds(block, length, stride=blocks), :] = upstream
    state_ref[rows_of(block)] = own_group(dot_split(ends, split(gated)))
    state_ref[rows_of(block + blocks)] = own_group(dot_split(starts, split(upstream)))


def send_states_kernel(*refs):
    sources, decay_hbm = refs[:4], refs[4]
    state_ref, rate_ref, gated_ref, upstream_ref, decay_ref = refs[5:10]
    sent, kept = refs[10:14], refs[14:18]
    table_ref, sems, decay_sem = refs[18:]
    half = kept_half(lax.axis_index("seq"))
    length, width = sent[0].shape
    blocks = width // LANES
    decay_copy = pltpu.make_async_copy(decay_hbm, decay_ref, decay_sem)
    decay_copy.start()
    copies = []
    for role, targets in enumerate([sent, kept]):
        at = pl.multiple_of((half if role else 1 - half) * width, width)
        for n in range(4):
            copy = pltpu.make_async_copy(
                sources[n].at[:, pl.ds(at, width)], targets[n], sems.at[role, n]
            )
            copies.append(copy)
    for copy in copies[:4]:
        copy.start()
    decay_copy.wait()
    for copy in copies[4:]:
        copy.start()
    decay = of_half(decay_ref[...], 1 - half)
    def make(block, place, first):
        rate, *powers = power_tables(turned(decay, first), place, length)
        rate_ref[rows_of(block)] = own_group(rate)
        for n, power in enumerate(powers):
            table_ref[2 * n, :, lanes_of(block)], table_ref[2 * n + 1, :, lanes_of(block)] = split(
                power
            )

    over_blocks(blocks, STEP, make)
    for copy in copies[:4]:
        copy.wait()

    def use(block, place, first):
        high, low, start_high, start_low = (table_ref[n, :, lanes_of(block)] for n in range(4))
        block_states(
            block,
            (high, low),
            (start_high, start_low),
            sent,
            state_ref,
            gated_ref,
            upstream_ref,
        )

    over_blocks(blocks, STEP, use)
    for copy in copies[4:]:
        copy.wait()


def keep_states_kernel(decay_ref, *refs):
    streams = refs[:4]
    state_ref, rate_ref, gated_ref, upstream_ref = refs[4:]
    decay = of_half(decay_ref[...], kept_half(lax.axis_index("seq")))
    length, width = streams[0].shape

    def both(block, place, first):
        rate, ends, starts = power_tables(turned(decay, first), place, length)
        rate_ref[rows_of(block)] = own_group(rate)
        block_states(
            block, split(ends), split(starts), streams, state_ref, gated_ref, upstream_ref
        )

    over_blocks(width // LANES, STEP, both)


def state_shapes(length, width):
    blocks = width // LANES
    return [
        ((2 * blocks * MODES, LANES), F32),
        ((blocks * MODES, LANES), F32),
        ((length * blocks, LANES), F32),
        ((length * blocks, LANES), F32),
    ]


def send_states(k, v, q, c, decay):
    length, total = k.shape
    arrays = [pltpu.with_memory_space_constraint(x, pltpu.HBM) for x in (k, v, q, c, decay)]
    outs = call(
        send_states_kernel,
        "send_states",
        state_shapes(length, total // 2)
        + [(decay.shape, F32)]
        + [((length, total // 2), k.dtype)] * 8,
        *arrays,
        scratch=[
            pltpu.VMEM((4, LANES, length * total // 2 // LANES), BF16),
            pltpu.SemaphoreType.DMA((2, 4)),
            pltpu.SemaphoreType.DMA,
        ],
        ins_in=[pltpu.HBM] * 5,
    )
    return outs[:4], outs[4], outs[5:9], outs[9:]


def keep_states(decay, streams):
    return call(
        keep_states_kernel, "keep_states", state_shapes(*streams[0].shape), decay, *streams
    )


def tables_kernel(keep, decay_ref, residue_ref, rate_ref, *refs):
    weight_ref, fh_ref, fl_ref, bh_ref, bl_ref = refs
    length, width = fh_ref.shape
    half = kept_half(lax.axis_index("seq"))
    weights = residue_ref[...] * jnp.sqrt(2.0 * decay_ref[...] / MODES)
    weights = of_half(weights, half if keep else 1 - half)
    pick = lane_iota((MODES, LANES)) % MODES == row_iota((MODES, LANES))
    time = row_iota((MODES, LANES)).astype(F32)

    def across(stack):
        return jnp.sum(jnp.where(pick, stack, 0.0), axis=0, keepdims=True)

    for block in range(width // LANES):
        lanes = lanes_of(block)
        weight = own_group(columns(weights, block * PACK))
        weight_ref[rows_of(block)] = weight
        rate = jnp.broadcast_to(across(rate_ref[rows_of(block)]), (MODES, LANES))
        weight = jnp.broadcast_to(across(weight), (MODES, LANES))
        step = jnp.exp(-rate * MODES)
        fore = weight * jnp.exp(-rate * (time + 1.0))
        back = weight * jnp.exp(-rate * (MODES - time))
        for i in range(length // MODES):
            rows = rows_of(i)
            fh_ref[rows, lanes], fl_ref[rows, lanes] = split(fore)
            rows = rows_of(length // MODES - 1 - i)
            bh_ref[rows, lanes], bl_ref[rows, lanes] = split(back)
            fore = fore * step
            back = back * step


def tables(keep, decay, residue, rate, length):
    width = rate.shape[0] // MODES * LANES
    return call(
        functools.partial(tables_kernel, keep),
        "tables",
        [(rate.shape, F32)] + [((length, width), BF16)] * 4,
        decay,
        residue,
        rate,
    )


def by_mode(stack_ref, blocks):
    return [stack_ref[pl.ds(n, blocks, stride=MODES), :] for n in range(MODES)]


def lag_kernel(keep, gated_ref, upstream_ref, rate_ref, *refs):
    *cross_refs, out_ref, stack_ref = refs
    blocks = rate_ref.shape[0] // MODES
    half = kept_half(lax.axis_index("seq"))
    offset = (half if keep else 1 - half) * blocks
    decays = [jnp.exp(-rate) for rate in by_mode(rate_ref, blocks)]
    out = jnp.zeros((MODES, LANES), F32)
    for cross_ref in cross_refs:
        out = filter_sums(cross_ref[...], offset)

    def step(i, carry):
        states, totals = list(carry[0]), list(carry[1])
        place = pl.ds(pl.multiple_of(i * blocks, blocks), blocks)
        gated, upstream = gated_ref[place], upstream_ref[place]
        for n in range(MODES):
            states[n] = states[n] * decays[n] + gated
            totals[n] = totals[n] + states[n] * upstream
        return tuple(states), tuple(totals)

    zeros = (jnp.zeros((blocks, LANES), F32),) * MODES
    steps = gated_ref.shape[0] // blocks
    _, totals = lax.fori_loop(0, steps, step, (zeros, zeros), unroll=UNROLL)
    for n in range(MODES):
        stack_ref[pl.ds(n, blocks, stride=MODES), :] = totals[n]
    out_ref[...] = out + filter_sums(stack_ref[...], offset)


def lag_part(keep, gated, upstream, rate, *cross):
    return call(
        functools.partial(lag_kernel, keep),
        "lag_part",
        [((MODES, LANES), F32)],
        gated,
        upstream,
        rate,
        *cross,
        scratch=[pltpu.VMEM(rate.shape, F32)],
    )[0]


def scan_kernel(reverses, *refs):
    for n, reverse in enumerate(reverses):
        in_ref, rate_ref, weight_ref = refs[3 * n : 3 * n + 3]
        out_ref = refs[3 * len(reverses) + n]
        blocks = rate_ref.shape[0] // MODES
        steps = in_ref.shape[0] // blocks
        decays = [jnp.exp(-rate) for rate in by_mode(rate_ref, blocks)]
        weights = by_mode(weight_ref, blocks)

        def step(
            i,
            states,
            reverse=reverse,
            steps=steps,
            blocks=blocks,
            decays=decays,
            weights=weights,
            in_ref=in_ref,
            out_ref=out_ref,
        ):
            at = steps - 1 - i if reverse else i
            place = pl.ds(pl.multiple_of(at * blocks, blocks), blocks)
            value = in_ref[place]
            states = [state * decay + value for state, decay in zip(states, decays)]
            terms = [state * weight for state, weight in zip(states, weights)]
            while len(terms) > 1:
                terms = [a + b for a, b in zip(terms[::2], terms[1::2])]
            first = at // 8 * (8 * blocks) + at % 8
            out_ref[pl.ds(first, blocks, stride=8), :] = terms[0]
            return tuple(states)

        zeros = (jnp.zeros((blocks, LANES), F32),) * MODES
        lax.fori_loop(0, steps, step, zeros, unroll=UNROLL)


def scan_part(tasks):
    return call(
        functools.partial(scan_kernel, [task[3] for task in tasks]),
        "scan",
        [(task[0].shape, F32) for task in tasks],
        *[x for task in tasks for x in task[:3]],
    )


UNROLL = 128


def join(own, other, late, power, step_decay):
    half = power.shape[0]
    own_end, own_start = own[:half], own[half : 2 * half]
    other_end, other_start = other[:half], other[half : 2 * half]
    early_end = jnp.where(late, other_end, own_end)
    late_end = jnp.where(late, own_end, other_end)
    early_start = jnp.where(late, other_start, own_start)
    late_start = jnp.where(late, own_start, other_start)
    end = late_end + power * early_end
    start = early_start + power * late_start
    return end, start, early_end * late_start * step_decay


def pass_down(first, second, before, after, power):
    early = (before, second + power * after)
    late = (first + power * before, after)
    return early, late


def quarter_of(index, ref):
    rows = ref.shape[0] // 2
    return pl.ds(pl.multiple_of(((index >> 1) & 1) * rows, rows), rows)


def first_block(index, rows):
    return (kept_half(index) * 2 + ((index >> 1) & 1)) * (rows // MODES)


def core_kernel(length, own_ref, other_ref, rate_ref, send_ref, keep_ref, cross_ref):
    index = lax.axis_index("seq")
    half = own_ref.shape[0] // 2
    quarter = half // 2
    rate = rate_ref[...]
    end, start, cross = join(
        own_ref[...],
        other_ref[...],
        bit_of(index, 1),
        jnp.exp(-rate * length),
        jnp.exp(-rate),
    )
    second = bit_of(index, 2)
    keep_ref[:quarter] = jnp.where(second, end[quarter:], end[:quarter])
    keep_ref[quarter:] = jnp.where(second, start[quarter:], start[:quarter])
    send_ref[:quarter] = jnp.where(second, end[:quarter], end[quarter:])
    send_ref[quarter:] = jnp.where(second, start[:quarter], start[quarter:])
    cross_ref[...] = cross


def core_join(length, own, other, rate):
    half = ((own.shape[0] // 2, LANES), F32)
    return call(
        functools.partial(core_kernel, length),
        "core_join",
        [half, half, half],
        own,
        other,
        rate,
    )


def plane_kernel(length, own_ref, other_ref, *refs):
    *sums_refs, rate_ref, out_ref = refs
    index = lax.axis_index("seq")
    quarter = own_ref.shape[0] // 2
    rate = rate_ref[quarter_of(index, rate_ref)]
    end, start, cross = join(
        own_ref[...],
        other_ref[...],
        bit_of(index, 2),
        jnp.exp(-rate * (2 * length)),
        jnp.exp(-rate),
    )
    out_ref[:quarter] = end
    out_ref[quarter : 2 * quarter] = start
    sums = filter_sums(cross, first_block(index, quarter))
    for ref in sums_refs:
        sums = sums + ref[...]
    out_ref[2 * quarter :] = sums


def plane_join(length, own, other, sums, rate):
    return call(
        functools.partial(plane_kernel, length),
        "plane_join",
        [((own.shape[0] + MODES, LANES), F32)],
        own,
        other,
        *sums,
        rate,
    )[0]


def line_kernel(length, mask, final, own_ref, other_ref, rate_ref, out_ref):
    index = lax.axis_index("seq")
    quarter = (own_ref.shape[0] - MODES) // 2
    rate = rate_ref[quarter_of(index, rate_ref)]
    end, start, cross = join(
        own_ref[...],
        other_ref[...],
        bit_of(index, mask),
        jnp.exp(-rate * (mask * length)),
        jnp.exp(-rate),
    )
    sums = own_ref[2 * quarter :] + other_ref[2 * quarter :] + filter_sums(cross, first_block(index, quarter))
    if final:
        out_ref[:quarter] = jnp.where(bit_of(index, 2 * mask), start, end)
        out_ref[quarter:] = sums
    else:
        out_ref[:quarter] = end
        out_ref[quarter : 2 * quarter] = start
        out_ref[2 * quarter :] = sums


def line_join(length, mask, final, own, other, rate):
    quarter = (own.shape[0] - MODES) // 2
    count = (quarter if final else 2 * quarter) + MODES
    return call(
        functools.partial(line_kernel, length, mask, final),
        "line_join",
        [((count, LANES), F32)],
        own,
        other,
        rate,
    )[0]


def turn_kernel(length, masks, own_ref, other_ref, *refs):
    levels = refs[: len(masks) - 1]
    chip_ref, chip_other_ref, rate_ref, keep_ref, send_ref = refs[len(masks) - 1 :]
    index = lax.axis_index("seq")
    quarter = own_ref.shape[0] - MODES
    rate = rate_ref[quarter_of(index, rate_ref)]
    own, other = own_ref[:quarter], other_ref[:quarter]
    late = bit_of(index, masks[-1])
    cross = own * other * jnp.exp(-rate)
    sums = own_ref[quarter:] + other_ref[quarter:] + filter_sums(cross, first_block(index, quarter))
    before = jnp.where(late, other, 0.0)
    after = jnp.where(late, 0.0, other)
    for mask, level in reversed(list(zip(masks[:-1], levels))):
        late = bit_of(index, mask)
        power = jnp.exp(-rate * (mask * length))
        before, after = (
            jnp.where(late, level[:quarter] + power * before, before),
            jnp.where(late, after, level[quarter : 2 * quarter] + power * after),
        )
    late = bit_of(index, 2)
    power = jnp.exp(-rate * (2 * length))
    early_end = jnp.where(late, chip_other_ref[:quarter], chip_ref[:quarter])
    late_start = jnp.where(late, chip_ref[quarter:], chip_other_ref[quarter:])
    early, later = pass_down(early_end, late_start, before, after, power)
    keep_ref[:quarter] = jnp.where(late, later[0], early[0])
    keep_ref[quarter : 2 * quarter] = jnp.where(late, later[1], early[1])
    keep_ref[2 * quarter :] = sums
    send_ref[:quarter] = jnp.where(late, early[0], later[0])
    send_ref[quarter : 2 * quarter] = jnp.where(late, early[1], later[1])
    send_ref[2 * quarter :] = sums


def turn(length, masks, own, other, levels, chip, chip_other, rate):
    shape = ((chip.shape[0] + MODES, LANES), F32)
    return call(
        functools.partial(turn_kernel, length, masks),
        "turn",
        [shape, shape],
        own,
        other,
        *levels,
        chip,
        chip_other,
        rate,
    )


def chip_kernel(length, own_ref, other_ref, core_ref, core_other_ref, rate_ref, keep_ref, send_ref):
    index = lax.axis_index("seq")
    quarter = (own_ref.shape[0] - MODES) // 2
    half = 2 * quarter
    rate = rate_ref[...]
    power = jnp.exp(-rate * length)
    second = bit_of(index, 2)
    own, other = own_ref[:half], other_ref[:half]
    left = jnp.where(second, other, own)
    right = jnp.where(second, own, other)
    before = jnp.concatenate([left[:quarter], right[:quarter]], axis=0)
    after = jnp.concatenate([left[quarter:], right[quarter:]], axis=0)
    late = bit_of(index, 1)
    early_end = jnp.where(late, core_other_ref[:half], core_ref[:half])
    late_start = jnp.where(late, core_ref[half:], core_other_ref[half:])
    early, later = pass_down(early_end, late_start, before, after, power)
    sums = own_ref[half:] + other_ref[half:]
    keep_ref[:half] = jnp.where(late, later[0], early[0])
    keep_ref[half : 2 * half] = jnp.where(late, later[1], early[1])
    keep_ref[2 * half :] = sums
    send_ref[:half] = jnp.where(late, early[0], later[0])
    send_ref[half : 2 * half] = jnp.where(late, early[1], later[1])
    send_ref[2 * half :] = sums


def chip_split(length, own, other, core, core_other, rate):
    shape = ((core.shape[0] + MODES, LANES), F32)
    return call(
        functools.partial(chip_kernel, length),
        "chip_split",
        [shape, shape],
        own,
        other,
        core,
        core_other,
        rate,
    )


def spread(state):
    same = lane_iota((LANES, LANES)) // PER == row_iota((LANES, LANES)) // MODES
    return jnp.where(same, jnp.concatenate([state] * PACK, axis=0), jnp.zeros((), state.dtype))


def carried(high_ref, low_ref, lanes, state):
    high, low = split(state)
    high, low = spread(high), spread(low)
    return dot_split((high_ref[:, lanes], low_ref[:, lanes]), (high, low))


CHUNKS = 4


def write_block(block, blocks, refs, results):
    around_ref, k_ref, v_ref, q_ref, c_ref, fh_ref, fl_ref, bh_ref, bl_ref = refs[:9]
    fore_ref, back_ref = refs[9:11]
    out_ref, query_ref, key_ref, value_ref = results
    lanes = lanes_of(block)
    tiles = range(block * 8, fore_ref.shape[0], 8 * blocks)

    def own(ref):
        return jnp.concatenate([ref[i : i + 8] for i in tiles], axis=0)

    before = around_ref[rows_of(block)]
    after = around_ref[rows_of(blocks + block)]
    mixed = own(fore_ref) + carried(fh_ref, fl_ref, lanes, before)
    out_ref[:, lanes] = (q_ref[:, lanes].astype(F32) * mixed).astype(BF16)
    query_ref[:, lanes] = (c_ref[:, lanes].astype(F32) * mixed).astype(BF16)
    grad = own(back_ref) + carried(bh_ref, bl_ref, lanes, after)
    key_ref[:, lanes] = (grad * v_ref[:, lanes].astype(F32)).astype(BF16)
    value_ref[:, lanes] = (grad * k_ref[:, lanes].astype(F32)).astype(BF16)


def keep_outputs_kernel(*refs):
    blocks = refs[1].shape[1] // LANES
    for block in range(blocks):
        write_block(block, blocks, refs[:-4], refs[-4:])


def keep_outputs(operands):
    shape = (operands[1].shape, BF16)
    return call(keep_outputs_kernel, "keep_outputs", [shape] * 4, *operands)


def sent_outputs_kernel(scale, *refs):
    kept, own_ref, decay_ref = refs[:4], refs[4], refs[5]
    targets, grad_ref = refs[-11:-7], refs[-7]
    scratch, kept_sems, sems = refs[-6:-2], refs[-2], refs[-1]
    refs = refs[6:-11]
    around_ref = refs[0]
    width = refs[1].shape[1]
    blocks = width // LANES
    half = kept_half(lax.axis_index("seq"))
    copies = []

    def send(sources, which, start, size, sems):
        at = pl.multiple_of(which * width + start, size)
        for n in range(4):
            copy = pltpu.make_async_copy(
                sources[n].at[:, pl.ds(start, size)], targets[n].at[:, pl.ds(at, size)], sems.at[n]
            )
            copy.start()
            copies.append(copy)

    send(kept, half, 0, width, kept_sems)
    each = blocks // CHUNKS
    for chunk in range(CHUNKS):
        for block in range(chunk * each, (chunk + 1) * each):
            write_block(block, blocks, refs, scratch)
        send(scratch, 1 - half, chunk * each * LANES, each * LANES, sems.at[chunk])
    base = 2 * blocks * MODES
    sums = own_ref[base:] + around_ref[base:]
    grad_ref[...] = sums * jnp.sqrt(2.0 * decay_ref[...] / MODES) * scale
    for copy in copies:
        copy.wait()


def sent_outputs(scale, kept, own, decay, operands):
    length, width = kept[0].shape
    return call(
        functools.partial(sent_outputs_kernel, scale),
        "sent_outputs",
        [((length, 2 * width), BF16)] * 4 + [(decay.shape, F32)],
        *kept,
        own,
        decay,
        *operands,
        scratch=[pltpu.VMEM((length, width), BF16)] * 4
        + [pltpu.SemaphoreType.DMA((4,)), pltpu.SemaphoreType.DMA((CHUNKS, 4))],
        outs_in=[pltpu.HBM] * 4 + [pltpu.VMEM],
    )


FILL = (1, 1, 2)


def tie(*values):
    return lax.optimization_barrier(values)


def per_device(query, key, value, cotangent, decay, residue):
    length, total = query.shape
    blocks = total // LANES // 2
    count = lax.axis_size("seq")
    masks = [1 << i for i in range(2, count.bit_length() - 1)]
    decay, residue = decay.T, residue.T

    def swap(array, mask):
        flip = mask | 1
        return lax.ppermute(array, "seq", [(i, i ^ flip) for i in range(count)])

    first, decay, sent, kept = send_states(key, value, query, cotangent, decay)
    core_send, rate_sent, gated_sent, upstream_sent = first
    core_send, decay, gated_sent, upstream_sent, *kept = tie(
        core_send, decay, gated_sent, upstream_sent, *kept
    )
    core_other = swap(core_send, 1)
    core, rate, gated, upstream = keep_states(decay, kept)
    core_other, core = tie(core_other, core)
    chip_send, chip, core_cross = core_join(length, core, core_other, rate)
    chip_send, gated, upstream, gated_sent = tie(chip_send, gated, upstream, gated_sent)
    chip_other = swap(chip_send, 2)
    lags = [
        lag_part(False, gated_sent, upstream_sent, rate_sent),
        lag_part(True, gated, upstream, rate, core_cross),
    ]
    message = plane_join(length, chip, chip_other, lags, rate)

    message, rate, rate_sent = tie(message, rate, rate_sent)
    weight, *table = tables(True, decay, residue, rate, length)
    weight_sent, *table_sent = tables(False, decay, residue, rate_sent, length)
    tasks = [
        (values, rates, weights, reverse)
        for rates, weights, pair in [
            (rate, weight, (gated, upstream)),
            (rate_sent, weight_sent, (gated_sent, upstream_sent)),
        ]
        for reverse, values in zip((False, True), pair)
    ]
    scans = []

    def fill(number, held, *more):
        todo = tasks[len(scans) : len(scans) + number]
        held, *values = tie(held, *[task[0] for task in todo])
        scans.extend(scan_part([(x, *task[1:]) for x, task in zip(values, todo)]))

        def after(arrived):
            arrived, *scans[-number:] = tie(arrived, *scans[-number:])
            if more:
                arrived, *_ = tie(arrived, *more)
            return arrived

        return held, after

    levels = []
    for mask in masks[:-1]:
        if mask == masks[0]:
            message, after = fill(FILL[0], message, table[0], table_sent[0])
            levels.append(after(swap(message, mask)))
        else:
            levels.append(swap(message, mask))
        message = line_join(length, mask, mask == masks[-2], message, levels[-1], rate)
    message, after = fill(FILL[1], message)
    top = after(swap(message, masks[-1]))
    keep, send = turn(length, masks, message, top, levels, chip, chip_other, rate)
    send, after = fill(FILL[2], send)
    arrived = after(swap(send, 2))
    own, send = chip_split(length, keep, arrived, core, core_other, rate)
    rest = len(tasks) - len(scans)
    if rest:
        send, after = fill(rest, send)
        other = after(swap(send, 1))
    else:
        other = swap(send, 1)
    scale = 1.0 / math.sqrt(length * count)
    cut = len(scans) // 2
    done = keep_outputs([own, *kept, *table, *scans[:cut]])
    *wide, grad = sent_outputs(scale, done, own, decay, [other, *sent, *table_sent, *scans[cut:]])
    return (*wide, grad.T)


def solution(mesh):
    rows = P(("grp", "seq"), None)
    return jax.shard_map(
        per_device,
        mesh=mesh,
        in_specs=(rows, rows, rows, rows, P(), P()),
        out_specs=(rows, rows, rows, rows, P("grp", None)),
        check_vma=False,
    )
```

```python
import functools
import math

import jax
import jax.numpy as jnp
from jax import lax
from jax.experimental import pallas as pl
from jax.experimental.pallas import tpu as pltpu
from jax.sharding import PartitionSpec as P

PER = 16
MODES = 16
LANES = 128
PACK = LANES // PER
F32 = jnp.float32
BF16 = jnp.bfloat16


def lane_iota(shape):
    return lax.broadcasted_iota(jnp.int32, shape, 1)


def row_iota(shape):
    return lax.broadcasted_iota(jnp.int32, shape, 0)


def split(value):
    high = value.astype(BF16)
    return high, (value - high.astype(F32)).astype(BF16)


def lanes_of(block):
    if isinstance(block, int):
        return slice(block * LANES, (block + 1) * LANES)
    return pl.ds(pl.multiple_of(block * LANES, LANES), LANES)


def rows_of(block):
    if isinstance(block, int):
        return slice(block * MODES, (block + 1) * MODES)
    return pl.ds(pl.multiple_of(block * MODES, MODES), MODES)


def over_blocks(count, step, body):
    if step == count:
        for block in range(count):
            body(block, block, 0)
        return

    def some(i, carry):
        for n in range(step):
            body(i * step + n, n, i * step)
        return carry

    lax.fori_loop(0, count // step, some, 0)


def turned(by_filter, block):
    if isinstance(block, int):
        return by_filter
    return pltpu.roll(by_filter, (LANES - block * PACK) % LANES, 1)


STEP = 8


def dot_split(left, right):
    return jnp.dot(
        jnp.concatenate([left[0], left[0], left[1]], axis=1),
        jnp.concatenate([right[0], right[1], right[0]], axis=0),
        preferred_element_type=F32,
    )


def own_group(stack):
    group = lane_iota((MODES, LANES)) // PER
    total = stack[rows_of(0)]
    for g in range(1, PACK):
        total = jnp.where(group == g, stack[rows_of(g)], total)
    return total


def columns(by_filter, first):
    return jnp.concatenate(
        [
            jnp.broadcast_to(by_filter[:, g : g + 1], (MODES, LANES))
            for g in range(first, first + PACK)
        ],
        axis=0,
    )


def filter_sums(stack, first):
    high, low = split(stack)
    spot = lane_iota((LANES, LANES)) % PACK == row_iota((LANES, LANES)) // PER
    spot = spot.astype(F32).astype(BF16)
    sums = jnp.dot(
        jnp.concatenate([high, low], axis=1),
        jnp.concatenate([spot, spot], axis=0),
        preferred_element_type=F32,
    )
    block = lane_iota((MODES, LANES)) // PACK - first
    total = jnp.zeros((MODES, LANES), F32)
    for i in range(stack.shape[0] // MODES):
        total = total + jnp.where(block == i, sums[rows_of(i)], 0.0)
    return total


def bit_of(index, mask):
    return (index & mask) != 0


def kept_half(index):
    for shift in (8, 4, 2, 1):
        index = index ^ (index >> shift)
    return index & 1


def call(kernel, name, outs, *operands, scratch=(), outs_in=None, ins_in=None):
    ins_in = ins_in or [pltpu.VMEM] * len(operands)
    outs_in = outs_in or [pltpu.VMEM] * len(outs)
    return pl.pallas_call(
        kernel,
        in_specs=[pl.BlockSpec(memory_space=space) for space in ins_in],
        out_specs=[pl.BlockSpec(memory_space=space) for space in outs_in],
        out_shape=[jax.ShapeDtypeStruct(shape, dtype) for shape, dtype in outs],
        scratch_shapes=list(scratch),
        compiler_params=pltpu.CompilerParams(vmem_limit_bytes=16 << 20),
        name=name,
    )(*operands)


def of_half(by_filter, half):
    return jnp.where(half == 0, by_filter, pltpu.roll(by_filter, LANES // 2, 1))


def power_tables(decay, block, length):
    time = lane_iota((LANES, length)).astype(F32)
    rate = columns(decay, block * PACK)
    return rate, jnp.exp(-rate * (length - 1.0 - time)), jnp.exp(-rate * time)


def block_states(block, ends, starts, streams, state_ref, gated_ref, upstream_ref):
    k_ref, v_ref, q_ref, c_ref = streams
    length, width = k_ref.shape
    blocks = width // LANES
    lanes = lanes_of(block)
    gated = k_ref[:, lanes].astype(F32) * v_ref[:, lanes].astype(F32)
    upstream = q_ref[:, lanes].astype(F32) * c_ref[:, lanes].astype(F32)
    gated_ref[pl.ds(block, length, stride=blocks), :] = gated
    upstream_ref[pl.ds(block, length, stride=blocks), :] = upstream
    state_ref[rows_of(block)] = own_group(dot_split(ends, split(gated)))
    state_ref[rows_of(block + blocks)] = own_group(dot_split(starts, split(upstream)))


def send_states_kernel(*refs):
    sources, decay_hbm = refs[:4], refs[4]
    state_ref, rate_ref, gated_ref, upstream_ref, decay_ref = refs[5:10]
    sent, kept = refs[10:14], refs[14:18]
    table_ref, sems, decay_sem = refs[18:]
    half = kept_half(lax.axis_index("seq"))
    length, width = sent[0].shape
    blocks = width // LANES
    decay_copy = pltpu.make_async_copy(decay_hbm, decay_ref, decay_sem)
    decay_copy.start()
    copies = []
    for role, targets in enumerate([sent, kept]):
        at = pl.multiple_of((half if role else 1 - half) * width, width)
        for n in range(4):
            copy = pltpu.make_async_copy(
                sources[n].at[:, pl.ds(at, width)], targets[n], sems.at[role, n]
            )
            copies.append(copy)
    for copy in copies[:4]:
        copy.start()
    decay_copy.wait()
    for copy in copies[4:]:
        copy.start()
    decay = of_half(decay_ref[...], 1 - half)
    def make(block, place, first):
        rate, *powers = power_tables(turned(decay, first), place, length)
        rate_ref[rows_of(block)] = own_group(rate)
        for n, power in enumerate(powers):
            table_ref[2 * n, :, lanes_of(block)], table_ref[2 * n + 1, :, lanes_of(block)] = split(
                power
            )

    over_blocks(blocks, STEP, make)
    for copy in copies[:4]:
        copy.wait()

    def use(block, place, first):
        high, low, start_high, start_low = (table_ref[n, :, lanes_of(block)] for n in range(4))
        block_states(
            block,
            (high, low),
            (start_high, start_low),
            sent,
            state_ref,
            gated_ref,
            upstream_ref,
        )

    over_blocks(blocks, STEP, use)
    for copy in copies[4:]:
        copy.wait()


def keep_states_kernel(decay_ref, *refs):
    streams = refs[:4]
    state_ref, rate_ref, gated_ref, upstream_ref = refs[4:]
    decay = of_half(decay_ref[...], kept_half(lax.axis_index("seq")))
    length, width = streams[0].shape

    def both(block, place, first):
        rate, ends, starts = power_tables(turned(decay, first), place, length)
        rate_ref[rows_of(block)] = own_group(rate)
        block_states(
            block, split(ends), split(starts), streams, state_ref, gated_ref, upstream_ref
        )

    over_blocks(width // LANES, STEP, both)


def state_shapes(length, width):
    blocks = width // LANES
    return [
        ((2 * blocks * MODES, LANES), F32),
        ((blocks * MODES, LANES), F32),
        ((length * blocks, LANES), F32),
        ((length * blocks, LANES), F32),
    ]


def send_states(k, v, q, c, decay):
    length, total = k.shape
    arrays = [pltpu.with_memory_space_constraint(x, pltpu.HBM) for x in (k, v, q, c, decay)]
    outs = call(
        send_states_kernel,
        "send_states",
        state_shapes(length, total // 2)
        + [(decay.shape, F32)]
        + [((length, total // 2), k.dtype)] * 8,
        *arrays,
        scratch=[
            pltpu.VMEM((4, LANES, length * total // 2 // LANES), BF16),
            pltpu.SemaphoreType.DMA((2, 4)),
            pltpu.SemaphoreType.DMA,
        ],
        ins_in=[pltpu.HBM] * 5,
    )
    return outs[:4], outs[4], outs[5:9], outs[9:]


def keep_states(decay, streams):
    return call(
        keep_states_kernel, "keep_states", state_shapes(*streams[0].shape), decay, *streams
    )


def tables_kernel(keep, decay_ref, residue_ref, rate_ref, *refs):
    weight_ref, fh_ref, fl_ref, bh_ref, bl_ref = refs
    length, width = fh_ref.shape
    half = kept_half(lax.axis_index("seq"))
    weights = residue_ref[...] * jnp.sqrt(2.0 * decay_ref[...] / MODES)
    weights = of_half(weights, half if keep else 1 - half)
    pick = lane_iota((MODES, LANES)) % MODES == row_iota((MODES, LANES))
    time = row_iota((MODES, LANES)).astype(F32)

    def across(stack):
        return jnp.sum(jnp.where(pick, stack, 0.0), axis=0, keepdims=True)

    for block in range(width // LANES):
        lanes = lanes_of(block)
        weight = own_group(columns(weights, block * PACK))
        weight_ref[rows_of(block)] = weight
        rate = jnp.broadcast_to(across(rate_ref[rows_of(block)]), (MODES, LANES))
        weight = jnp.broadcast_to(across(weight), (MODES, LANES))
        step = jnp.exp(-rate * MODES)
        fore = weight * jnp.exp(-rate * (time + 1.0))
        back = weight * jnp.exp(-rate * (MODES - time))
        for i in range(length // MODES):
            rows = rows_of(i)
            fh_ref[rows, lanes], fl_ref[rows, lanes] = split(fore)
            rows = rows_of(length // MODES - 1 - i)
            bh_ref[rows, lanes], bl_ref[rows, lanes] = split(back)
            fore = fore * step
            back = back * step


def tables(keep, decay, residue, rate, length):
    width = rate.shape[0] // MODES * LANES
    return call(
        functools.partial(tables_kernel, keep),
        "tables",
        [(rate.shape, F32)] + [((length, width), BF16)] * 4,
        decay,
        residue,
        rate,
    )


def by_mode(stack_ref, blocks):
    return [stack_ref[pl.ds(n, blocks, stride=MODES), :] for n in range(MODES)]


def lag_kernel(*refs):
    *half_refs, cross_ref, out_ref, stack_ref = refs
    kept = kept_half(lax.axis_index("seq"))
    blocks = half_refs[2].shape[0] // MODES
    rows = blocks * MODES
    out = filter_sums(cross_ref[...], kept * blocks)
    for role, half in enumerate((1 - kept, kept)):
        gated_ref, upstream_ref, rate_ref = half_refs[3 * role : 3 * role + 3]
        decays = [jnp.exp(-rate) for rate in by_mode(rate_ref, blocks)]

        def step(i, carry, gated_ref=gated_ref, upstream_ref=upstream_ref, decays=decays):
            states, totals = list(carry[0]), list(carry[1])
            place = pl.ds(pl.multiple_of(i * blocks, blocks), blocks)
            gated, upstream = gated_ref[place], upstream_ref[place]
            for n in range(MODES):
                states[n] = states[n] * decays[n] + gated
                totals[n] = totals[n] + states[n] * upstream
            return tuple(states), tuple(totals)

        zeros = (jnp.zeros((blocks, LANES), F32),) * MODES
        steps = gated_ref.shape[0] // blocks
        _, totals = lax.fori_loop(0, steps, step, (zeros, zeros), unroll=UNROLL)
        for n in range(MODES):
            stack_ref[pl.ds(role * rows + n, blocks, stride=MODES), :] = totals[n]
        out = out + filter_sums(stack_ref[role * rows : (role + 1) * rows], half * blocks)
    out_ref[...] = out


def lag_part(sent, kept, cross):
    rows, lanes = cross.shape
    return call(
        lag_kernel,
        "lag_part",
        [((MODES, LANES), F32)],
        *sent,
        *kept,
        cross,
        scratch=[pltpu.VMEM((2 * rows, lanes), F32)],
    )[0]


def scan_kernel(reverses, *refs):
    for n, reverse in enumerate(reverses):
        in_ref, rate_ref, weight_ref = refs[3 * n : 3 * n + 3]
        out_ref = refs[3 * len(reverses) + n]
        blocks = rate_ref.shape[0] // MODES
        steps = in_ref.shape[0] // blocks
        decays = [jnp.exp(-rate) for rate in by_mode(rate_ref, blocks)]
        weights = by_mode(weight_ref, blocks)

        def step(
            i,
            states,
            reverse=reverse,
            steps=steps,
            blocks=blocks,
            decays=decays,
            weights=weights,
            in_ref=in_ref,
            out_ref=out_ref,
        ):
            at = steps - 1 - i if reverse else i
            place = pl.ds(pl.multiple_of(at * blocks, blocks), blocks)
            value = in_ref[place]
            states = [state * decay + value for state, decay in zip(states, decays)]
            terms = [state * weight for state, weight in zip(states, weights)]
            while len(terms) > 1:
                terms = [a + b for a, b in zip(terms[::2], terms[1::2])]
            first = at // 8 * (8 * blocks) + at % 8
            out_ref[pl.ds(first, blocks, stride=8), :] = terms[0]
            return tuple(states)

        zeros = (jnp.zeros((blocks, LANES), F32),) * MODES
        lax.fori_loop(0, steps, step, zeros, unroll=UNROLL)


def scan_part(tasks):
    return call(
        functools.partial(scan_kernel, [task[3] for task in tasks]),
        "scan",
        [(task[0].shape, F32) for task in tasks],
        *[x for task in tasks for x in task[:3]],
    )


UNROLL = 128


def join(own, other, late, power, step_decay):
    half = power.shape[0]
    own_end, own_start = own[:half], own[half : 2 * half]
    other_end, other_start = other[:half], other[half : 2 * half]
    early_end = jnp.where(late, other_end, own_end)
    late_end = jnp.where(late, own_end, other_end)
    early_start = jnp.where(late, other_start, own_start)
    late_start = jnp.where(late, own_start, other_start)
    end = late_end + power * early_end
    start = early_start + power * late_start
    return end, start, early_end * late_start * step_decay


def pass_down(first, second, before, after, power):
    early = (before, second + power * after)
    late = (first + power * before, after)
    return early, late


def quarter_of(index, ref):
    rows = ref.shape[0] // 2
    return pl.ds(pl.multiple_of(((index >> 1) & 1) * rows, rows), rows)


def first_block(index, rows):
    return (kept_half(index) * 2 + ((index >> 1) & 1)) * (rows // MODES)


def core_kernel(length, own_ref, other_ref, rate_ref, send_ref, keep_ref, cross_ref):
    index = lax.axis_index("seq")
    half = own_ref.shape[0] // 2
    quarter = half // 2
    rate = rate_ref[...]
    end, start, cross = join(
        own_ref[...],
        other_ref[...],
        bit_of(index, 1),
        jnp.exp(-rate * length),
        jnp.exp(-rate),
    )
    second = bit_of(index, 2)
    keep_ref[:quarter] = jnp.where(second, end[quarter:], end[:quarter])
    keep_ref[quarter:] = jnp.where(second, start[quarter:], start[:quarter])
    send_ref[:quarter] = jnp.where(second, end[:quarter], end[quarter:])
    send_ref[quarter:] = jnp.where(second, start[:quarter], start[quarter:])
    cross_ref[...] = cross


def core_join(length, own, other, rate):
    half = ((own.shape[0] // 2, LANES), F32)
    return call(
        functools.partial(core_kernel, length),
        "core_join",
        [half, half, half],
        own,
        other,
        rate,
    )


def plane_kernel(length, own_ref, other_ref, *refs):
    *sums_refs, rate_ref, out_ref = refs
    index = lax.axis_index("seq")
    quarter = own_ref.shape[0] // 2
    rate = rate_ref[quarter_of(index, rate_ref)]
    end, start, cross = join(
        own_ref[...],
        other_ref[...],
        bit_of(index, 2),
        jnp.exp(-rate * (2 * length)),
        jnp.exp(-rate),
    )
    out_ref[:quarter] = end
    out_ref[quarter : 2 * quarter] = start
    sums = filter_sums(cross, first_block(index, quarter))
    for ref in sums_refs:
        sums = sums + ref[...]
    out_ref[2 * quarter :] = sums


def plane_join(length, own, other, sums, rate):
    return call(
        functools.partial(plane_kernel, length),
        "plane_join",
        [((own.shape[0] + MODES, LANES), F32)],
        own,
        other,
        *sums,
        rate,
    )[0]


def line_kernel(length, mask, final, own_ref, other_ref, rate_ref, out_ref):
    index = lax.axis_index("seq")
    quarter = (own_ref.shape[0] - MODES) // 2
    rate = rate_ref[quarter_of(index, rate_ref)]
    end, start, cross = join(
        own_ref[...],
        other_ref[...],
        bit_of(index, mask),
        jnp.exp(-rate * (mask * length)),
        jnp.exp(-rate),
    )
    sums = own_ref[2 * quarter :] + other_ref[2 * quarter :] + filter_sums(cross, first_block(index, quarter))
    if final:
        out_ref[:quarter] = jnp.where(bit_of(index, 2 * mask), start, end)
        out_ref[quarter:] = sums
    else:
        out_ref[:quarter] = end
        out_ref[quarter : 2 * quarter] = start
        out_ref[2 * quarter :] = sums


def line_join(length, mask, final, own, other, rate):
    quarter = (own.shape[0] - MODES) // 2
    count = (quarter if final else 2 * quarter) + MODES
    return call(
        functools.partial(line_kernel, length, mask, final),
        "line_join",
        [((count, LANES), F32)],
        own,
        other,
        rate,
    )[0]


def turn_kernel(length, masks, own_ref, other_ref, *refs):
    levels = refs[: len(masks) - 1]
    chip_ref, chip_other_ref, rate_ref, keep_ref, send_ref = refs[len(masks) - 1 :]
    index = lax.axis_index("seq")
    quarter = own_ref.shape[0] - MODES
    rate = rate_ref[quarter_of(index, rate_ref)]
    own, other = own_ref[:quarter], other_ref[:quarter]
    late = bit_of(index, masks[-1])
    cross = own * other * jnp.exp(-rate)
    sums = own_ref[quarter:] + other_ref[quarter:] + filter_sums(cross, first_block(index, quarter))
    before = jnp.where(late, other, 0.0)
    after = jnp.where(late, 0.0, other)
    for mask, level in reversed(list(zip(masks[:-1], levels))):
        late = bit_of(index, mask)
        power = jnp.exp(-rate * (mask * length))
        before, after = (
            jnp.where(late, level[:quarter] + power * before, before),
            jnp.where(late, after, level[quarter : 2 * quarter] + power * after),
        )
    late = bit_of(index, 2)
    power = jnp.exp(-rate * (2 * length))
    early_end = jnp.where(late, chip_other_ref[:quarter], chip_ref[:quarter])
    late_start = jnp.where(late, chip_ref[quarter:], chip_other_ref[quarter:])
    early, later = pass_down(early_end, late_start, before, after, power)
    keep_ref[:quarter] = jnp.where(late, later[0], early[0])
    keep_ref[quarter : 2 * quarter] = jnp.where(late, later[1], early[1])
    keep_ref[2 * quarter :] = sums
    send_ref[:quarter] = jnp.where(late, early[0], later[0])
    send_ref[quarter : 2 * quarter] = jnp.where(late, early[1], later[1])
    send_ref[2 * quarter :] = sums


def turn(length, masks, own, other, levels, chip, chip_other, rate):
    shape = ((chip.shape[0] + MODES, LANES), F32)
    return call(
        functools.partial(turn_kernel, length, masks),
        "turn",
        [shape, shape],
        own,
        other,
        *levels,
        chip,
        chip_other,
        rate,
    )


def chip_kernel(length, own_ref, other_ref, core_ref, core_other_ref, rate_ref, keep_ref, send_ref):
    index = lax.axis_index("seq")
    quarter = (own_ref.shape[0] - MODES) // 2
    half = 2 * quarter
    rate = rate_ref[...]
    power = jnp.exp(-rate * length)
    second = bit_of(index, 2)
    own, other = own_ref[:half], other_ref[:half]
    left = jnp.where(second, other, own)
    right = jnp.where(second, own, other)
    before = jnp.concatenate([left[:quarter], right[:quarter]], axis=0)
    after = jnp.concatenate([left[quarter:], right[quarter:]], axis=0)
    late = bit_of(index, 1)
    early_end = jnp.where(late, core_other_ref[:half], core_ref[:half])
    late_start = jnp.where(late, core_ref[half:], core_other_ref[half:])
    early, later = pass_down(early_end, late_start, before, after, power)
    sums = own_ref[half:] + other_ref[half:]
    keep_ref[:half] = jnp.where(late, later[0], early[0])
    keep_ref[half : 2 * half] = jnp.where(late, later[1], early[1])
    keep_ref[2 * half :] = sums
    send_ref[:half] = jnp.where(late, early[0], later[0])
    send_ref[half : 2 * half] = jnp.where(late, early[1], later[1])
    send_ref[2 * half :] = sums


def chip_split(length, own, other, core, core_other, rate):
    shape = ((core.shape[0] + MODES, LANES), F32)
    return call(
        functools.partial(chip_kernel, length),
        "chip_split",
        [shape, shape],
        own,
        other,
        core,
        core_other,
        rate,
    )


def spread(state):
    same = lane_iota((LANES, LANES)) // PER == row_iota((LANES, LANES)) // MODES
    return jnp.where(same, jnp.concatenate([state] * PACK, axis=0), jnp.zeros((), state.dtype))


def carried(high_ref, low_ref, lanes, state):
    high, low = split(state)
    high, low = spread(high), spread(low)
    return dot_split((high_ref[:, lanes], low_ref[:, lanes]), (high, low))


CHUNKS = 4


def write_block(block, blocks, refs, results):
    around_ref, k_ref, v_ref, q_ref, c_ref, fh_ref, fl_ref, bh_ref, bl_ref = refs[:9]
    fore_ref, back_ref = refs[9:11]
    out_ref, query_ref, key_ref, value_ref = results
    lanes = lanes_of(block)
    tiles = range(block * 8, fore_ref.shape[0], 8 * blocks)

    def own(ref):
        return jnp.concatenate([ref[i : i + 8] for i in tiles], axis=0)

    before = around_ref[rows_of(block)]
    after = around_ref[rows_of(blocks + block)]
    mixed = own(fore_ref) + carried(fh_ref, fl_ref, lanes, before)
    out_ref[:, lanes] = (q_ref[:, lanes].astype(F32) * mixed).astype(BF16)
    query_ref[:, lanes] = (c_ref[:, lanes].astype(F32) * mixed).astype(BF16)
    grad = own(back_ref) + carried(bh_ref, bl_ref, lanes, after)
    key_ref[:, lanes] = (grad * v_ref[:, lanes].astype(F32)).astype(BF16)
    value_ref[:, lanes] = (grad * k_ref[:, lanes].astype(F32)).astype(BF16)


def keep_outputs_kernel(*refs):
    blocks = refs[1].shape[1] // LANES
    for block in range(blocks):
        write_block(block, blocks, refs[:-4], refs[-4:])


def keep_outputs(operands):
    shape = (operands[1].shape, BF16)
    return call(keep_outputs_kernel, "keep_outputs", [shape] * 4, *operands)


def sent_outputs_kernel(scale, *refs):
    kept, own_ref, decay_ref = refs[:4], refs[4], refs[5]
    targets, grad_ref = refs[-11:-7], refs[-7]
    scratch, kept_sems, sems = refs[-6:-2], refs[-2], refs[-1]
    refs = refs[6:-11]
    around_ref = refs[0]
    width = refs[1].shape[1]
    blocks = width // LANES
    half = kept_half(lax.axis_index("seq"))
    copies = []

    def send(sources, which, start, size, sems):
        at = pl.multiple_of(which * width + start, size)
        for n in range(4):
            copy = pltpu.make_async_copy(
                sources[n].at[:, pl.ds(start, size)], targets[n].at[:, pl.ds(at, size)], sems.at[n]
            )
            copy.start()
            copies.append(copy)

    send(kept, half, 0, width, kept_sems)
    each = blocks // CHUNKS
    for chunk in range(CHUNKS):
        for block in range(chunk * each, (chunk + 1) * each):
            write_block(block, blocks, refs, scratch)
        send(scratch, 1 - half, chunk * each * LANES, each * LANES, sems.at[chunk])
    base = 2 * blocks * MODES
    sums = own_ref[base:] + around_ref[base:]
    grad_ref[...] = sums * jnp.sqrt(2.0 * decay_ref[...] / MODES) * scale
    for copy in copies:
        copy.wait()


def sent_outputs(scale, kept, own, decay, operands):
    length, width = kept[0].shape
    return call(
        functools.partial(sent_outputs_kernel, scale),
        "sent_outputs",
        [((length, 2 * width), BF16)] * 4 + [(decay.shape, F32)],
        *kept,
        own,
        decay,
        *operands,
        scratch=[pltpu.VMEM((length, width), BF16)] * 4
        + [pltpu.SemaphoreType.DMA((4,)), pltpu.SemaphoreType.DMA((CHUNKS, 4))],
        outs_in=[pltpu.HBM] * 4 + [pltpu.VMEM],
    )


FILL = (1, 1, 2)


def tie(*values):
    return lax.optimization_barrier(values)


def per_device(query, key, value, cotangent, decay, residue):
    length, total = query.shape
    blocks = total // LANES // 2
    count = lax.axis_size("seq")
    masks = [1 << i for i in range(2, count.bit_length() - 1)]
    decay, residue = decay.T, residue.T

    def swap(array, mask):
        flip = mask | 1
        return lax.ppermute(array, "seq", [(i, i ^ flip) for i in range(count)])

    first, decay, sent, kept = send_states(key, value, query, cotangent, decay)
    core_send, rate_sent, gated_sent, upstream_sent = first
    core_send, decay, gated_sent, upstream_sent, *kept = tie(
        core_send, decay, gated_sent, upstream_sent, *kept
    )
    core_other = swap(core_send, 1)
    core, rate, gated, upstream = keep_states(decay, kept)
    core_other, core = tie(core_other, core)
    chip_send, chip, core_cross = core_join(length, core, core_other, rate)
    chip_send, gated, upstream, gated_sent = tie(chip_send, gated, upstream, gated_sent)
    chip_other = swap(chip_send, 2)
    lags = [
        lag_part(
            (gated_sent, upstream_sent, rate_sent), (gated, upstream, rate), core_cross
        )
    ]
    message = plane_join(length, chip, chip_other, lags, rate)

    message, rate, rate_sent = tie(message, rate, rate_sent)
    weight, *table = tables(True, decay, residue, rate, length)
    weight_sent, *table_sent = tables(False, decay, residue, rate_sent, length)
    tasks = [
        (values, rates, weights, reverse)
        for rates, weights, pair in [
            (rate, weight, (gated, upstream)),
            (rate_sent, weight_sent, (gated_sent, upstream_sent)),
        ]
        for reverse, values in zip((False, True), pair)
    ]
    scans = []

    def fill(number, held, *more):
        todo = tasks[len(scans) : len(scans) + number]
        held, *values = tie(held, *[task[0] for task in todo])
        scans.extend(scan_part([(x, *task[1:]) for x, task in zip(values, todo)]))

        def after(arrived):
            arrived, *scans[-number:] = tie(arrived, *scans[-number:])
            if more:
                arrived, *_ = tie(arrived, *more)
            return arrived

        return held, after

    levels = []
    for mask in masks[:-1]:
        if mask == masks[0]:
            message, after = fill(FILL[0], message, table[0], table_sent[0])
            levels.append(after(swap(message, mask)))
        else:
            levels.append(swap(message, mask))
        message = line_join(length, mask, mask == masks[-2], message, levels[-1], rate)
    message, after = fill(FILL[1], message)
    top = after(swap(message, masks[-1]))
    keep, send = turn(length, masks, message, top, levels, chip, chip_other, rate)
    send, after = fill(FILL[2], send)
    arrived = after(swap(send, 2))
    own, send = chip_split(length, keep, arrived, core, core_other, rate)
    rest = len(tasks) - len(scans)
    if rest:
        send, after = fill(rest, send)
        other = after(swap(send, 1))
    else:
        other = swap(send, 1)
    scale = 1.0 / math.sqrt(length * count)
    cut = len(scans) // 2
    done = keep_outputs([own, *kept, *table, *scans[:cut]])
    *wide, grad = sent_outputs(scale, done, own, decay, [other, *sent, *table_sent, *scans[cut:]])
    return (*wide, grad.T)


def solution(mesh):
    rows = P(("grp", "seq"), None)
    return jax.shard_map(
        per_device,
        mesh=mesh,
        in_specs=(rows, rows, rows, rows, P(), P()),
        out_specs=(rows, rows, rows, rows, P("grp", None)),
        check_vma=False,
    )
```
